512 devices in a mesh: ctx: 64 (over y, z), head: 8 (over x, core).
Axes of the slice: x: 4, y: 4, z: 16, core: 2. Of those that a mesh axis runs over, the one named last changes fastest.
Arguments:
- query_rows: bfloat16 [32768, 2048], P('ctx', 'head'), parts along dimension 1, may hold values from -6 to 6
- key_rows: bfloat16 [32768, 2048], P('ctx', 'head'), parts along dimension 1, may hold values from -6 to 6
- value_rows: bfloat16 [32768, 2048], P('ctx', 'head'), parts along dimension 1, may hold values from -6 to 6
- out_grad: bfloat16 [32768, 2048], P('ctx', 'head'), parts along dimension 1, may hold values from -6 to 6
- doc_lengths: int32 [64], P('head'), parts along dimension 0, may hold values from 1 to 8192, 32768 in all
Outputs:
- attended: bfloat16 [32768, 2048], P('ctx', 'head'), parts along dimension 1
- grad_query: bfloat16 [32768, 2048], P('ctx', 'head'), parts along dimension 1
- grad_key: bfloat16 [32768, 2048], P('ctx', 'head'), parts along dimension 1
- grad_value: bfloat16 [32768, 2048], P('ctx', 'head'), parts along dimension 1
The draws below stay inside these ranges and needn't reach their ends.
There are 8 independent parts, one for each index of `head`. The reference program is written for one: setup_inputs(seed, part) draws one part's arguments, and reference() takes and returns one part's arrays. A program takes and returns all parts, laid end to end along the dimension named above; each array names one. Nothing has to cross between parts.
Inputs may be any that keep to these rules, and one draw needn't show every extreme that they name: `doc_lengths`: the lengths add up to 32768; the longest document holds exactly 8192 tokens.
All inputs are finite; a program needn't handle non-finite values.
Results may differ from the reference program's by a relative error of at most 0.0051.
Values sent between devices are 32-bit elements; how exact they have to be, the bound alone decides.
A program may use at most 64 MiB of HBM per device.

```python
import math
import jax
import jax.numpy as jnp
import numpy as np
from jax import lax

HD = 128
HEADS = 2
TOK_DEV = 512
DOCS = 8
TOKENS = 32768
DOC_MOST = 8192
N_CTX = 64


def steps_of(rng, shape, cuts, smallest, largest):
    loudness, own = 1.0, jax.random.fold_in(rng, 6)
    for axis_at, blocks in cuts:
        draws = jnp.exp(jax.random.uniform(jax.random.fold_in(own, axis_at), (blocks,), jnp.float32, smallest / len(cuts), largest / len(cuts)))
        loudness = loudness * jnp.repeat(draws, shape[axis_at] // blocks).reshape([-1 if axis == axis_at else 1 for axis in range(len(shape))])
    return loudness


def split_up(number_of, total, bound, lean):
    portions = [(1 << 20) // math.isqrt(rank ** lean) + 1 for rank in range(2, number_of + 1)]
    spare, given = total - bound - (number_of - 1), [1] * (number_of - 1)
    while spare > 0:
        free = [i for i in range(number_of - 1) if given[i] < bound]
        mass, budget = sum([portions[i] for i in free]), spare
        for i in free:
            addition = min(bound - given[i], max(1, budget * portions[i] // mass), spare)
            given[i] = given[i] + addition
            spare = spare - addition
    return np.array([bound] + given)


def ragged(rng, count, total, bound, skew):
    if count == 2:
        one = jax.random.randint(rng, (), max(1, total - bound), min(bound, total - 1) + 1)
        return jnp.stack([one, total - one])
    lengths = jnp.asarray(split_up(count, total, bound, skew), jnp.int32)
    pairs = (count - 1) // 2
    donor, sink = lengths[1:1 + 2 * pairs:2], lengths[2:2 + 2 * pairs:2]
    room = jnp.minimum(donor - 1, bound - sink)
    shifted = jax.random.randint(jax.random.fold_in(rng, 1), (pairs,), 0, 1 << 20) % (room + 1)
    lengths = lengths.at[1:1 + 2 * pairs:2].set(donor - shifted).at[2:2 + 2 * pairs:2].set(sink + shifted)
    return lengths[jax.random.permutation(jax.random.fold_in(rng, 2), count)]


def scatter_about(own_key, extent, deviation, limit, pieces=(), kind=jnp.bfloat16):
    drawn = deviation * jax.random.normal(own_key, extent, jnp.float32)
    if pieces:
        drawn = drawn * steps_of(own_key, extent, pieces, -0.22, 0.18)
    return jnp.clip(drawn, -limit, limit).astype(kind)


def setup_inputs(seed: int = 0, part: int = 0) -> dict:
    streams_of = jax.random.split(jax.random.key(seed), 6)
    part_splits = jax.random.split(jax.random.fold_in(streams_of[5], part), 6)
    return {
        "query_rows": scatter_about(part_splits[0], (TOKENS, HEADS * HD), 1.0, 6.0, ((0, 64),)),
        "key_rows": scatter_about(part_splits[1], (TOKENS, HEADS * HD), 1.0, 6.0, ((0, 64),)),
        "value_rows": scatter_about(part_splits[2], (TOKENS, HEADS * HD), 1.0, 6.0, ((0, 64),)),
        "out_grad": scatter_about(part_splits[3], (TOKENS, HEADS * HD), 1.0, 6.0, ((0, 64),)),
        "doc_lengths": ragged(part_splits[4], DOCS, TOKENS, DOC_MOST, 2).astype(jnp.int32),
    }


def doc_layout(doc_lengths, base, rows):
    count = doc_lengths.shape[0]
    lengths_int = doc_lengths.astype(jnp.int32)
    starts = (jnp.cumsum(lengths_int) - lengths_int).astype(jnp.int32)
    finish = (starts + lengths_int).astype(jnp.int32)
    positions = (base + jnp.arange(rows, dtype=jnp.int32)).astype(jnp.int32)
    member = ((positions[:, None] >= starts[None, :]) & (positions[:, None] < finish[None, :])).astype(jnp.int32)
    labels = jnp.arange(count, dtype=jnp.int32)
    doc_index = lax.optimization_barrier(jnp.sum(member * labels[None, :], axis=1)).astype(jnp.int32)
    offsets = (positions - lax.optimization_barrier(jnp.sum(member * starts[None, :], axis=1))).astype(jnp.int32)
    first_doc = doc_index[0]
    last_doc = doc_index[rows - 1]
    first_start = jnp.sum(jnp.where(labels == first_doc, starts, 0))
    last_start = jnp.sum(jnp.where(labels == last_doc, starts, 0))
    first_finish = jnp.sum(jnp.where(labels == first_doc, finish, 0))
    last_finish = jnp.sum(jnp.where(labels == last_doc, finish, 0))
    carry_in = (first_start < base).astype(jnp.float32)
    reset_fwd = (last_start >= base).astype(jnp.float32)
    reset_bwd = (first_finish <= base + rows).astype(jnp.float32)
    carry_back = (last_finish > base + rows).astype(jnp.float32)
    local = jnp.arange(rows, dtype=jnp.int32)
    allowed = (doc_index[:, None] == doc_index[None, :]) & (local[:, None] >= local[None, :])
    return (offsets, doc_index == first_doc, doc_index == last_doc, carry_in, reset_fwd, reset_bwd, carry_back, allowed)

def scale_rows(offsets):
    return lax.rsqrt(offsets.astype(jnp.float32) + 1.0) * HD ** (-0.5)

def reference(query_rows, key_rows, value_rows, out_grad, doc_lengths):
    hi = lax.Precision.HIGHEST
    shape = (N_CTX, TOK_DEV, HEADS, HD)
    query_blk = query_rows.reshape(shape)
    key_blk = key_rows.reshape(shape)
    value_blk = value_rows.reshape(shape)
    grad_blk = out_grad.reshape(shape)
    block_ids = jnp.arange(N_CTX, dtype=jnp.int32)
    zero_state = jnp.zeros((HEADS, HD, HD), jnp.float32)

    def forward_step(carry, inputs):
        block_no, key_part, value_part = inputs
        layout = doc_layout(doc_lengths, block_no * TOK_DEV, TOK_DEV)
        last_rows = layout[2]
        kept = jnp.where(last_rows[:, None, None], key_part, jnp.zeros_like(key_part)).astype(jnp.float32)
        tail_state = jnp.einsum('thd,the->hde', kept, value_part.astype(jnp.float32), precision=hi)
        entering = carry * layout[3]
        return (tail_state + (1.0 - layout[4]) * carry, entering)

    def backward_step(carry, inputs):
        block_no, query_part, grad_part = inputs
        layout = doc_layout(doc_lengths, block_no * TOK_DEV, TOK_DEV)
        row_scale = scale_rows(layout[0])
        scaled = (query_part.astype(jnp.float32) * row_scale[:, None, None]).astype(jnp.bfloat16)
        kept = jnp.where(layout[1][:, None, None], scaled, jnp.zeros_like(scaled)).astype(jnp.float32)
        head_state = jnp.einsum('thd,the->hde', kept, grad_part.astype(jnp.float32), precision=hi)
        returning = carry * layout[6]
        return (head_state + (1.0 - layout[5]) * carry, returning)
    final_fwd, entering_all = lax.scan(forward_step, zero_state, (block_ids, key_blk, value_blk))
    final_bwd, returning_all = lax.scan(backward_step, zero_state, (block_ids, query_blk, grad_blk), reverse=True)

    def block_work(inputs):
        block_no, query_part, key_part, value_part, grad_part, entering, returning = inputs
        layout = doc_layout(doc_lengths, block_no * TOK_DEV, TOK_DEV)
        row_scale = scale_rows(layout[0])
        allowed = layout[7][None, :, :]
        scaled = (query_part.astype(jnp.float32) * row_scale[:, None, None]).astype(jnp.bfloat16)
        scaled_f = scaled.astype(jnp.float32)
        key_f = key_part.astype(jnp.float32)
        value_f = value_part.astype(jnp.float32)
        grad_f = grad_part.astype(jnp.float32)
        scores = jnp.einsum('thd,shd->hts', scaled_f, key_f, precision=hi)
        weights = jnp.where(allowed, scores, 0.0).astype(jnp.bfloat16).astype(jnp.float32)
        attended = jnp.einsum('thd,hde->the', scaled_f, entering, precision=hi) + jnp.einsum('hts,she->the', weights, value_f, precision=hi)
        dscores = jnp.einsum('the,she->hts', grad_f, value_f, precision=hi)
        dweights = jnp.where(allowed, dscores, 0.0).astype(jnp.bfloat16).astype(jnp.float32)
        grad_q = row_scale[:, None, None] * (jnp.einsum('the,hde->thd', grad_f, entering, precision=hi) + jnp.einsum('hts,shd->thd', dweights, key_f, precision=hi))
        grad_k = jnp.einsum('she,hde->shd', value_f, returning, precision=hi) + jnp.einsum('hts,thd->shd', dweights, scaled_f, precision=hi)
        grad_v = jnp.einsum('shd,hde->she', key_f, returning, precision=hi) + jnp.einsum('hts,the->she', weights, grad_f, precision=hi)
        return (attended.astype(jnp.bfloat16), grad_q.astype(jnp.bfloat16), grad_k.astype(jnp.bfloat16), grad_v.astype(jnp.bfloat16))
    results = lax.map(block_work, (block_ids, query_blk, key_blk, value_blk, grad_blk, entering_all, returning_all))
    flat = (TOKENS, HEADS * HD)
    return (results[0].reshape(flat), results[1].reshape(flat), results[2].reshape(flat), results[3].reshape(flat))
```

```python
import functools

import jax
import jax.numpy as jnp
from jax import lax
from jax.experimental import pallas as pl
from jax.experimental.pallas import tpu as pltpu
from jax.sharding import PartitionSpec as P

HD = 128
HEADS = 2
ROWS = 512
DOCS = 8
BLOCKS = 64
GROUP = 4
GROUPS = BLOCKS // GROUP
REACH = 4
PIECES = 4
PROWS = HEADS * HD // PIECES
MESH = pl.DeviceIdType.MESH
F32 = jnp.float32
BF16 = jnp.bfloat16
TN = (((0,), (0,)), ((), ()))
NT = (((1,), (1,)), ((), ()))
NN = (((1,), (0,)), ((), ()))


def dot(a, b, dims):
    return lax.dot_general(a, b, dims, preferred_element_type=F32)


def flag(cond):
    return jnp.where(cond, jnp.float32(1.0), jnp.float32(0.0))


def owner(group, piece):
    turned = (group % 4) // 2
    return piece + turned * (3 - 2 * piece)


def split(x):
    hi = x.astype(BF16)
    return hi, (x - hi.astype(F32)).astype(BF16)


def kernel(
    dl_ref, q_ref, k_ref, v_ref, g_ref, att_ref, gq_ref, gk_ref, gv_ref,
    state, near_in, far_out, far_in, back_out, back_in, scaled_s, acc,
    ss1, rs1, ss2, rs2, ss3, rs3,
):
    c = lax.axis_index("ctx")
    h = lax.axis_index("head")
    grp = c // GROUP
    me = c % GROUP
    piece = owner(grp, me)

    def member(i):
        return (grp * GROUP + i, h)

    def far(step):
        other = (grp + step + GROUPS) % GROUPS
        return (other * GROUP + owner(other, piece), h)

    barrier = pltpu.get_barrier_semaphore()
    partners = [member((me + d) % GROUP) for d in range(1, GROUP)]
    partners += [far(s * d) for d in range(1, REACH + 1) for s in (1, -1)]
    for p in partners:
        pl.semaphore_signal(barrier, inc=1, device_id=p, device_id_type=MESH)

    starts, ends = [], []
    total = jnp.int32(0)
    for d in range(DOCS):
        starts.append(total)
        total = total + dl_ref[d]
        ends.append(total)

    def start_of(pos):
        best = jnp.int32(0)
        for d in range(1, DOCS):
            best = jnp.where(starts[d] <= pos, starts[d], best)
        return best

    def end_of(pos):
        best = ends[DOCS - 1]
        for d in range(DOCS - 2, -1, -1):
            best = jnp.where(ends[d] > pos, ends[d], best)
        return best

    base = c * ROWS
    last_start = start_of(base + ROWS - 1)
    first_end = end_of(base)
    pos = base + lax.broadcasted_iota(jnp.int32, (ROWS, HD), 0)
    doc_start = jnp.zeros((ROWS, HD), jnp.int32)
    for d in range(1, DOCS):
        doc_start = jnp.where(pos >= starts[d], starts[d], doc_start)
    row_scale = lax.rsqrt((pos - doc_start).astype(F32) + 1.0) * HD ** (-0.5)
    in_last = pos >= last_start
    in_first = pos < first_end

    for hd in range(HEADS):
        cols = slice(hd * HD, (hd + 1) * HD)
        tail = jnp.where(in_last, k_ref[:, cols].astype(F32), 0.0).astype(BF16)
        st = dot(tail, v_ref[:, cols], TN)
        state[2 * hd, 0] = st[:PROWS]
        state[2 * hd + 1, 0] = st[PROWS:]
        sc = q_ref[:, cols].astype(F32) * row_scale
        scaled_s[:, cols] = sc.astype(BF16)
        head = jnp.where(in_first, sc, 0.0).astype(BF16)
        st = dot(head, g_ref[:, cols], TN)
        state[2 * hd, 1] = st[:PROWS]
        state[2 * hd + 1, 1] = st[PROWS:]

    pl.semaphore_wait(barrier, len(partners))

    def near_copy(i, slot):
        return pltpu.make_async_remote_copy(
            state.at[owner(grp, i)], near_in.at[slot], ss1.at[i], rs1.at[slot],
            device_id=member(i), device_id_type=MESH)

    for d in range(1, GROUP):
        near_copy((me + d) % GROUP, me).start()
    near_in[me] = state[piece]

    def local_work(hd):
        cols = slice(hd * HD, (hd + 1) * HD)
        half = ROWS // 2
        for tb in range(2):
            rows = slice(tb * half, (tb + 1) * half)
            width = (tb + 1) * half
            sc, gr = scaled_s[rows, cols], g_ref[rows, cols]
            ke, va = k_ref[:width, cols], v_ref[:width, cols]
            col = base + lax.broadcasted_iota(jnp.int32, (half, width), 1)
            row = base + tb * half + lax.broadcasted_iota(jnp.int32, (half, width), 0)
            first = jnp.tile(doc_start[rows], (1, width // HD))
            allowed = (col <= row) & (col >= first)
            w = jnp.where(allowed, dot(sc, ke, NT), 0.0).astype(BF16)
            dw = jnp.where(allowed, dot(gr, va, NT), 0.0).astype(BF16)
            acc[0, rows, cols] = dot(w, va, NN)
            acc[1, rows, cols] = dot(dw, ke, NN)
            gk, gv = dot(dw, sc, TN), dot(w, gr, TN)
            if tb == 0:
                acc[2, rows, cols] = gk
                acc[3, rows, cols] = gv
            else:
                acc[2, :half, cols] += gk[:half]
                acc[3, :half, cols] += gv[:half]
                acc[2, half:, cols] = gk[half:]
                acc[3, half:, cols] = gv[half:]

    local_work(0)

    for d in range(1, GROUP):
        i = (me + d) % GROUP
        near_copy(i, i).wait_recv()

    block0 = grp * GROUP
    gbase = block0 * ROWS
    glast_start = start_of(gbase + GROUP * ROWS - 1)
    gfirst_end = end_of(gbase)
    tail_total = near_in[GROUP - 1, 0]
    head_total = near_in[0, 1]
    for i in range(GROUP - 1):
        tail_total += flag(glast_start < gbase + (i + 1) * ROWS) * near_in[i, 0]
        head_total += flag(gfirst_end > gbase + (i + 1) * ROWS) * near_in[i + 1, 1]
    far_out[0] = tail_total
    far_out[1] = head_total

    def far_copy(scan, d):
        return pltpu.make_async_remote_copy(
            far_out.at[scan], far_in.at[scan, d - 1], ss2.at[scan, d - 1], rs2.at[scan, d - 1],
            device_id=far(d if scan == 0 else -d), device_id_type=MESH)

    for d in (2, 3, 1, 4):
        for scan in range(2):
            far_copy(scan, d).start()

    local_work(1)

    for d in range(1, REACH + 1):
        for scan in range(2):
            far_copy(scan, d).wait_recv()

    gfirst_start = start_of(gbase)
    glast_end = end_of(gbase + GROUP * ROWS - 1)
    from_left = flag(gfirst_start < gbase) * far_in[0, 0]
    from_right = flag(glast_end > gbase + GROUP * ROWS) * far_in[1, 0]
    for d in range(2, REACH + 1):
        from_left += flag(gfirst_start < gbase - (d - 1) * GROUP * ROWS) * far_in[0, d - 1]
        from_right += flag(glast_end > gbase + d * GROUP * ROWS) * far_in[1, d - 1]
    for i in range(GROUP):
        at = gbase + i * ROWS
        begin = start_of(at)
        finish = end_of(at + ROWS - 1)
        entering = flag(begin < gbase) * from_left
        for r in range(i):
            entering += flag(begin < gbase + (r + 1) * ROWS) * near_in[r, 0]
        returning = flag(finish > gbase + GROUP * ROWS) * from_right
        for r in range(i + 1, GROUP):
            returning += flag(finish > gbase + r * ROWS) * near_in[r, 1]
        back_out[i, 0] = entering
        back_out[i, 1] = returning

    def back_copy(i, slot):
        return pltpu.make_async_remote_copy(
            back_out.at[i], back_in.at[slot], ss3.at[i], rs3.at[slot],
            device_id=member(i), device_id_type=MESH)

    for d in range(1, GROUP):
        back_copy((me + d) % GROUP, piece).start()
    back_in[piece] = back_out[me]
    for d in range(1, GROUP):
        i = (me + d) % GROUP
        back_copy(i, owner(grp, i)).wait_recv()

    for hd in range(HEADS):
        cols = slice(hd * HD, (hd + 1) * HD)
        e_hi, e_lo = split(jnp.concatenate([back_in[2 * hd, 0], back_in[2 * hd + 1, 0]], axis=0))
        r_hi, r_lo = split(jnp.concatenate([back_in[2 * hd, 1], back_in[2 * hd + 1, 1]], axis=0))
        sc, gr, ke, va = scaled_s[:, cols], g_ref[:, cols], k_ref[:, cols], v_ref[:, cols]
        att = acc[0, :, cols] + dot(sc, e_hi, NN) + dot(sc, e_lo, NN)
        att_ref[:, cols] = att.astype(BF16)
        gq = acc[1, :, cols] + dot(gr, e_hi, NT) + dot(gr, e_lo, NT)
        gq_ref[:, cols] = (row_scale * gq).astype(BF16)
        gk = acc[2, :, cols] + dot(va, r_hi, NT) + dot(va, r_lo, NT)
        gk_ref[:, cols] = gk.astype(BF16)
        gv = acc[3, :, cols] + dot(ke, r_hi, NN) + dot(ke, r_lo, NN)
        gv_ref[:, cols] = gv.astype(BF16)

    for d in range(1, GROUP):
        i = (me + d) % GROUP
        near_copy(i, i).wait_send()
        back_copy(i, i).wait_send()
    for d in range(1, REACH + 1):
        for scan in range(2):
            far_copy(scan, d).wait_send()


def body(query_rows, key_rows, value_rows, out_grad, doc_lengths):
    vmem = pl.BlockSpec(memory_space=pltpu.VMEM)
    out = jax.ShapeDtypeStruct((ROWS, HEADS * HD), BF16)
    dma = pltpu.SemaphoreType.DMA
    return pl.pallas_call(
        kernel,
        out_shape=(out,) * 4,
        in_specs=[pl.BlockSpec(memory_space=pltpu.SMEM)] + [vmem] * 4,
        out_specs=(vmem,) * 4,
        scratch_shapes=[
            pltpu.VMEM((PIECES, 2, PROWS, HD), F32),
            pltpu.VMEM((GROUP, 2, PROWS, HD), F32),
            pltpu.VMEM((2, PROWS, HD), F32),
            pltpu.VMEM((2, REACH, PROWS, HD), F32),
            pltpu.VMEM((GROUP, 2, PROWS, HD), F32),
            pltpu.VMEM((PIECES, 2, PROWS, HD), F32),
            pltpu.VMEM((ROWS, HEADS * HD), BF16),
            pltpu.VMEM((4, ROWS, HEADS * HD), F32),
            dma((GROUP,)), dma((GROUP,)), dma((2, REACH)), dma((2, REACH)), dma((GROUP,)), dma((GROUP,)),
        ],
        compiler_params=pltpu.CompilerParams(
            collective_id=0, has_side_effects=True, vmem_limit_bytes=48 * 1024 * 1024),
        name="linear_attention",
    )(doc_lengths, query_rows, key_rows, value_rows, out_grad)


def solution(mesh):
    in_specs = (P("ctx", "head"), P("ctx", "head"), P("ctx", "head"), P("ctx", "head"), P("head"))
    out_specs = (P("ctx", "head"), P("ctx", "head"), P("ctx", "head"), P("ctx", "head"))
    return jax.shard_map(body, mesh=mesh, in_specs=in_specs, out_specs=out_specs, check_vma=False)
```

```python
import functools

import jax
import jax.numpy as jnp
from jax import lax
from jax.experimental import pallas as pl
from jax.experimental.pallas import tpu as pltpu
from jax.sharding import PartitionSpec as P

HD = 128
HEADS = 2
ROWS = 512
DOCS = 8
BLOCKS = 64
GROUP = 4
GROUPS = BLOCKS // GROUP
REACH = 4
GROUP_COLS = 4
COLUMNS = (2, 3, 1, 0)
PIECES = 4
PROWS = HEADS * HD // PIECES
MESH = pl.DeviceIdType.MESH
F32 = jnp.float32
BF16 = jnp.bfloat16
TN = (((0,), (0,)), ((), ()))
NT = (((1,), (1,)), ((), ()))
NN = (((1,), (0,)), ((), ()))


def dot(a, b, dims):
    return lax.dot_general(a, b, dims, preferred_element_type=F32)


def flag(cond):
    return jnp.where(cond, jnp.float32(1.0), jnp.float32(0.0))


def owner(group, piece):
    turned = (group % 4) // 2
    return piece + turned * (3 - 2 * piece)


def split(x):
    hi = x.astype(BF16)
    return hi, (x - hi.astype(F32)).astype(BF16)


def kernel(
    dl_hbm, q_hbm, k_hbm, v_hbm, g_hbm, att_ref, gq_ref, gk_ref, gv_ref,
    dl_ref, q_ref, k_ref, v_ref, g_ref,
    state, near_in, far_out, far_in, back_out, back_in, scaled_s, acc,
    ld, ss1, rs1, ss2, rs2, ss3, rs3,
):
    loads = [
        pltpu.make_async_copy(src, dst, ld.at[i])
        for i, (src, dst) in enumerate(
            [(dl_hbm, dl_ref), (k_hbm, k_ref), (v_hbm, v_ref), (q_hbm, q_ref), (g_hbm, g_ref)])
    ]
    for load in loads:
        load.start()

    c = lax.axis_index("ctx")
    h = lax.axis_index("head")
    grp = c // GROUP
    me = c % GROUP
    piece = owner(grp, me)

    def member(i):
        return (grp * GROUP + i, h)

    def far(step):
        other = (grp + step + GROUPS) % GROUPS
        return (other * GROUP + owner(other, piece), h)

    barrier = pltpu.get_barrier_semaphore()
    partners = [member((me + d) % GROUP) for d in range(1, GROUP)]
    partners += [far(s * d) for d in range(1, REACH + 1) for s in (1, -1)]
    for p in partners:
        pl.semaphore_signal(barrier, inc=1, device_id=p, device_id_type=MESH)

    loads[0].wait()
    starts, ends = [], []
    total = jnp.int32(0)
    for d in range(DOCS):
        starts.append(total)
        total = total + dl_ref[d]
        ends.append(total)

    def start_of(pos):
        best = jnp.int32(0)
        for d in range(1, DOCS):
            best = jnp.where(starts[d] <= pos, starts[d], best)
        return best

    def end_of(pos):
        best = ends[DOCS - 1]
        for d in range(DOCS - 2, -1, -1):
            best = jnp.where(ends[d] > pos, ends[d], best)
        return best

    base = c * ROWS
    last_start = start_of(base + ROWS - 1)
    first_end = end_of(base)
    pos = base + lax.broadcasted_iota(jnp.int32, (ROWS, HD), 0)
    doc_start = jnp.zeros((ROWS, HD), jnp.int32)
    for d in range(1, DOCS):
        doc_start = jnp.where(pos >= starts[d], starts[d], doc_start)
    row_scale = lax.rsqrt((pos - doc_start).astype(F32) + 1.0) * HD ** (-0.5)
    in_last = pos >= last_start
    in_first = pos < first_end

    def near_copy(scan, i, slot):
        return pltpu.make_async_remote_copy(
            state.at[scan, owner(grp, i)], near_in.at[scan, slot], ss1.at[scan, i], rs1.at[scan, slot],
            device_id=member(i), device_id_type=MESH)

    def near_send(scan):
        for d in (2, 3, 1):
            near_copy(scan, (me + d) % GROUP, me).start()
        near_in[scan, me] = state[scan, piece]

    def near_wait(scan):
        for d in (1, 2, 3):
            i = (me + d) % GROUP
            near_copy(scan, i, i).wait_recv()

    loads[1].wait()
    loads[2].wait()
    for hd in range(HEADS):
        cols = slice(hd * HD, (hd + 1) * HD)
        tail = jnp.where(in_last, k_ref[:, cols].astype(F32), 0.0).astype(BF16)
        st = dot(tail, v_ref[:, cols], TN)
        state[0, 2 * hd] = st[:PROWS]
        state[0, 2 * hd + 1] = st[PROWS:]
    pl.semaphore_wait(barrier, len(partners))
    near_send(0)

    loads[3].wait()
    loads[4].wait()
    for hd in range(HEADS):
        cols = slice(hd * HD, (hd + 1) * HD)
        sc = q_ref[:, cols].astype(F32) * row_scale
        scaled_s[:, cols] = sc.astype(BF16)
        head = jnp.where(in_first, sc, 0.0).astype(BF16)
        st = dot(head, g_ref[:, cols], TN)
        state[1, 2 * hd] = st[:PROWS]
        state[1, 2 * hd + 1] = st[PROWS:]
    near_send(1)

    def local_work(hd):
        cols = slice(hd * HD, (hd + 1) * HD)
        half = ROWS // 2
        for tb in range(2):
            rows = slice(tb * half, (tb + 1) * half)
            width = (tb + 1) * half
            sc, gr = scaled_s[rows, cols], g_ref[rows, cols]
            ke, va = k_ref[:width, cols], v_ref[:width, cols]
            col = base + lax.broadcasted_iota(jnp.int32, (half, width), 1)
            row = base + tb * half + lax.broadcasted_iota(jnp.int32, (half, width), 0)
            first = jnp.tile(doc_start[rows], (1, width // HD))
            allowed = (col <= row) & (col >= first)
            w = jnp.where(allowed, dot(sc, ke, NT), 0.0).astype(BF16)
            dw = jnp.where(allowed, dot(gr, va, NT), 0.0).astype(BF16)
            acc[0, rows, cols] = dot(w, va, NN)
            acc[1, rows, cols] = dot(dw, ke, NN)
            gk, gv = dot(dw, sc, TN), dot(w, gr, TN)
            if tb == 0:
                acc[2, rows, cols] = gk
                acc[3, rows, cols] = gv
            else:
                acc[2, :half, cols] += gk[:half]
                acc[3, :half, cols] += gv[:half]
                acc[2, half:, cols] = gk[half:]
                acc[3, half:, cols] = gv[half:]

    local_work(0)

    block0 = grp * GROUP
    gbase = block0 * ROWS
    gend = gbase + GROUP * ROWS
    col = grp % GROUP_COLS
    glast_start = start_of(gend - 1)
    gfirst_end = end_of(gbase)

    def far_copy(scan, d):
        return pltpu.make_async_remote_copy(
            far_out.at[scan], far_in.at[scan, d - 1], ss2.at[scan, d - 1], rs2.at[scan, d - 1],
            device_id=far(d if scan == 0 else -d), device_id_type=MESH)

    def far_send(scan, columns):
        for t in columns:
            step = t - col if scan == 0 else col - t
            far_copy(scan, (step + 2 * GROUP_COLS - 1) % GROUP_COLS + 1).start()

    near_wait(0)
    total = near_in[0, GROUP - 1]
    for i in range(GROUP - 1):
        total += flag(glast_start < gbase + (i + 1) * ROWS) * near_in[0, i]
    far_out[0] = total
    far_send(0, COLUMNS[:2])

    near_wait(1)
    total = near_in[1, 0]
    for i in range(1, GROUP):
        total += flag(gfirst_end > gbase + i * ROWS) * near_in[1, i]
    far_out[1] = total
    far_send(1, COLUMNS[:2])
    far_send(0, COLUMNS[2:])
    far_send(1, COLUMNS[2:])

    local_work(1)

    gfirst_start = start_of(gbase)
    glast_end = end_of(gend - 1)

    def back_copy(scan, i, slot):
        return pltpu.make_async_remote_copy(
            back_out.at[scan, i], back_in.at[scan, slot], ss3.at[scan, i], rs3.at[scan, slot],
            device_id=member(i), device_id_type=MESH)

    def back_send(scan):
        for d in (2, 3, 1):
            back_copy(scan, (me + d) % GROUP, piece).start()
        back_in[scan, piece] = back_out[scan, me]

    def back_wait(scan):
        for d in (1, 2, 3):
            i = (me + d) % GROUP
            back_copy(scan, i, owner(grp, i)).wait_recv()

    for d in range(1, REACH + 1):
        far_copy(0, d).wait_recv()
    outer = flag(gfirst_start < gbase) * far_in[0, 0]
    for d in range(2, REACH + 1):
        outer += flag(gfirst_start < gbase - (d - 1) * GROUP * ROWS) * far_in[0, d - 1]
    for i in range(GROUP):
        begin = start_of(gbase + i * ROWS)
        entering = flag(begin < gbase) * outer
        for r in range(i):
            entering += flag(begin < gbase + (r + 1) * ROWS) * near_in[0, r]
        back_out[0, i] = entering
    back_send(0)

    for d in range(1, REACH + 1):
        far_copy(1, d).wait_recv()
    outer = flag(glast_end > gend) * far_in[1, 0]
    for d in range(2, REACH + 1):
        outer += flag(glast_end > gbase + d * GROUP * ROWS) * far_in[1, d - 1]
    for i in range(GROUP):
        finish = end_of(gbase + (i + 1) * ROWS - 1)
        returning = flag(finish > gend) * outer
        for r in range(i + 1, GROUP):
            returning += flag(finish > gbase + r * ROWS) * near_in[1, r]
        back_out[1, i] = returning
    back_send(1)

    back_wait(0)
    for hd in range(HEADS):
        cols = slice(hd * HD, (hd + 1) * HD)
        e_hi, e_lo = split(jnp.concatenate([back_in[0, 2 * hd], back_in[0, 2 * hd + 1]], axis=0))
        sc, gr = scaled_s[:, cols], g_ref[:, cols]
        att = acc[0, :, cols] + dot(sc, e_hi, NN) + dot(sc, e_lo, NN)
        att_ref[:, cols] = att.astype(BF16)
        gq = acc[1, :, cols] + dot(gr, e_hi, NT) + dot(gr, e_lo, NT)
        gq_ref[:, cols] = (row_scale * gq).astype(BF16)
    back_wait(1)
    for hd in range(HEADS):
        cols = slice(hd * HD, (hd + 1) * HD)
        r_hi, r_lo = split(jnp.concatenate([back_in[1, 2 * hd], back_in[1, 2 * hd + 1]], axis=0))
        ke, va = k_ref[:, cols], v_ref[:, cols]
        gk = acc[2, :, cols] + dot(va, r_hi, NT) + dot(va, r_lo, NT)
        gk_ref[:, cols] = gk.astype(BF16)
        gv = acc[3, :, cols] + dot(ke, r_hi, NN) + dot(ke, r_lo, NN)
        gv_ref[:, cols] = gv.astype(BF16)

    for scan in range(2):
        for d in range(1, GROUP):
            i = (me + d) % GROUP
            near_copy(scan, i, i).wait_send()
            back_copy(scan, i, i).wait_send()
        for d in range(1, REACH + 1):
            far_copy(scan, d).wait_send()


def writer(*refs):
    srcs, dsts, sem = refs[:4], refs[4:8], refs[8]
    copies = [pltpu.make_async_copy(a, b, sem.at[i]) for i, (a, b) in enumerate(zip(srcs, dsts))]
    for copy in copies:
        copy.start()
    for copy in copies:
        copy.wait()


def body(query_rows, key_rows, value_rows, out_grad, doc_lengths):
    vmem = pl.BlockSpec(memory_space=pltpu.VMEM)
    out = jax.ShapeDtypeStruct((ROWS, HEADS * HD), BF16)
    dma = pltpu.SemaphoreType.DMA
    hbm = pl.BlockSpec(memory_space=pltpu.HBM)
    rows = pltpu.VMEM((ROWS, HEADS * HD), BF16)
    results = pl.pallas_call(
        kernel,
        out_shape=(pltpu.VMEM((ROWS, HEADS * HD), BF16),) * 4,
        in_specs=[hbm] * 5,
        out_specs=(vmem,) * 4,
        scratch_shapes=[
            pltpu.SMEM((DOCS,), jnp.int32), rows, rows, rows, rows,
            pltpu.VMEM((2, PIECES, PROWS, HD), F32),
            pltpu.VMEM((2, GROUP, PROWS, HD), F32),
            pltpu.VMEM((2, PROWS, HD), F32),
            pltpu.VMEM((2, REACH, PROWS, HD), F32),
            pltpu.VMEM((2, GROUP, PROWS, HD), F32),
            pltpu.VMEM((2, PIECES, PROWS, HD), F32),
            pltpu.VMEM((ROWS, HEADS * HD), BF16),
            pltpu.VMEM((4, ROWS, HEADS * HD), F32),
            dma((5,)), dma((2, GROUP)), dma((2, GROUP)), dma((2, REACH)), dma((2, REACH)),
            dma((2, GROUP)), dma((2, GROUP)),
        ],
        compiler_params=pltpu.CompilerParams(
            collective_id=0, has_side_effects=True),
        name="linear_attention",
    )(doc_lengths, query_rows, key_rows, value_rows, out_grad)
    return pl.pallas_call(
        writer,
        out_shape=(out,) * 4,
        in_specs=[vmem] * 4,
        out_specs=(hbm,) * 4,
        scratch_shapes=[dma((4,))],
        name="write_out",
    )(*[pltpu.with_memory_space_constraint(x, pltpu.VMEM) for x in results])


def solution(mesh):
    in_specs = (P("ctx", "head"), P("ctx", "head"), P("ctx", "head"), P("ctx", "head"), P("head"))
    out_specs = (P("ctx", "head"), P("ctx", "head"), P("ctx", "head"), P("ctx", "head"))
    return jax.shard_map(body, mesh=mesh, in_specs=in_specs, out_specs=out_specs, check_vma=False)
```

```python
import functools

import jax
import jax.numpy as jnp
from jax import lax
from jax.experimental import pallas as pl
from jax.experimental.pallas import tpu as pltpu
from jax.sharding import PartitionSpec as P

HD = 128
HEADS = 2
ROWS = 512
DOCS = 8
BLOCKS = 64
GROUP = 4
GROUPS = BLOCKS // GROUP
REACH = 4
GROUP_COLS = 4
FAR = [(scan, d) for d in range(1, REACH + 1) for scan in range(2)]
PIECES = 4
PROWS = HEADS * HD // PIECES
MESH = pl.DeviceIdType.MESH
F32 = jnp.float32
BF16 = jnp.bfloat16
TN = (((0,), (0,)), ((), ()))
NT = (((1,), (1,)), ((), ()))
NN = (((1,), (0,)), ((), ()))


def dot(a, b, dims):
    return lax.dot_general(a, b, dims, preferred_element_type=F32)


def flag(cond):
    return jnp.where(cond, jnp.float32(1.0), jnp.float32(0.0))


def owner(group, piece):
    turned = (group % 4) // 2
    return piece + turned * (3 - 2 * piece)


def entry_order(group):
    column = group % GROUP_COLS
    place = column + (column // 2) * (5 - 2 * column)
    return place * (GROUPS // GROUP_COLS) + group // GROUP_COLS


def split(x):
    hi = x.astype(BF16)
    return hi, (x - hi.astype(F32)).astype(BF16)


def kernel(
    dl_hbm, q_hbm, k_hbm, v_hbm, g_hbm, att_ref, gq_ref, gk_ref, gv_ref,
    dl_ref, q_ref, k_ref, v_ref, g_ref,
    state, near_in, far_out, far_in, back_out, back_in, scaled_s, acc,
    ld, ready, ss1, rs1, ss2, rs2, ss3, rs3,
):
    loads = [
        pltpu.make_async_copy(src, dst, ld.at[i])
        for i, (src, dst) in enumerate(
            [(dl_hbm, dl_ref), (k_hbm, k_ref), (v_hbm, v_ref), (q_hbm, q_ref), (g_hbm, g_ref)])
    ]
    for load in loads:
        load.start()

    c = lax.axis_index("ctx")
    h = lax.axis_index("head")
    grp = c // GROUP
    me = c % GROUP
    piece = owner(grp, me)

    def member(i):
        return (grp * GROUP + i, h)

    def far(step):
        other = (grp + step + GROUPS) % GROUPS
        return (other * GROUP + owner(other, piece), h)

    def after(step):
        other = (grp + step + GROUPS) % GROUPS
        return jnp.where(entry_order(other) > entry_order(grp), 1, 0)

    later = [[after(d if scan == 0 else -d) for d in range(1, REACH + 1)] for scan in range(2)]

    barrier = pltpu.get_barrier_semaphore()
    awaited = jnp.int32(GROUP - 1)
    for d in range(1, GROUP):
        pl.semaphore_signal(barrier, inc=1, device_id=member((me + d) % GROUP), device_id_type=MESH)
    for scan, d in FAR:
        awaited = awaited + 1 - later[scan][d - 1]

        @pl.when(later[scan][d - 1] == 1)
        def _():
            pl.semaphore_signal(
                barrier, inc=1, device_id=far(d if scan == 0 else -d), device_id_type=MESH)

    loads[0].wait()
    starts, ends = [], []
    total = jnp.int32(0)
    for d in range(DOCS):
        starts.append(total)
        total = total + dl_ref[d]
        ends.append(total)

    def start_of(pos):
        best = jnp.int32(0)
        for d in range(1, DOCS):
            best = jnp.where(starts[d] <= pos, starts[d], best)
        return best

    def end_of(pos):
        best = ends[DOCS - 1]
        for d in range(DOCS - 2, -1, -1):
            best = jnp.where(ends[d] > pos, ends[d], best)
        return best

    base = c * ROWS
    last_start = start_of(base + ROWS - 1)
    first_end = end_of(base)
    pos = base + lax.broadcasted_iota(jnp.int32, (ROWS, HD), 0)
    doc_start = jnp.zeros((ROWS, HD), jnp.int32)
    for d in range(1, DOCS):
        doc_start = jnp.where(pos >= starts[d], starts[d], doc_start)
    row_scale = lax.rsqrt((pos - doc_start).astype(F32) + 1.0) * HD ** (-0.5)
    in_last = pos >= last_start
    in_first = pos < first_end

    def near_copy(scan, i, slot):
        return pltpu.make_async_remote_copy(
            state.at[scan, owner(grp, i)], near_in.at[scan, slot], ss1.at[scan, i], rs1.at[scan, slot],
            device_id=member(i), device_id_type=MESH)

    def near_send(scan):
        for d in (2, 3, 1):
            near_copy(scan, (me + d) % GROUP, me).start()
        near_in[scan, me] = state[scan, piece]

    def near_wait(scan):
        for d in (1, 2, 3):
            i = (me + d) % GROUP
            near_copy(scan, i, i).wait_recv()

    loads[1].wait()
    loads[2].wait()
    for hd in range(HEADS):
        cols = slice(hd * HD, (hd + 1) * HD)
        tail = jnp.where(in_last, k_ref[:, cols].astype(F32), 0.0).astype(BF16)
        st = dot(tail, v_ref[:, cols], TN)
        state[0, 2 * hd] = st[:PROWS]
        state[0, 2 * hd + 1] = st[PROWS:]
    pl.semaphore_wait(barrier, awaited)
    near_send(0)
    for scan, d in FAR:
        @pl.when(later[scan][d - 1] == 0)
        def _():
            pl.semaphore_signal(
                ready.at[1 - scan, d - 1], inc=1,
                device_id=far(d if scan == 0 else -d), device_id_type=MESH)

    loads[3].wait()
    loads[4].wait()
    for hd in range(HEADS):
        cols = slice(hd * HD, (hd + 1) * HD)
        sc = q_ref[:, cols].astype(F32) * row_scale
        scaled_s[:, cols] = sc.astype(BF16)
        head = jnp.where(in_first, sc, 0.0).astype(BF16)
        st = dot(head, g_ref[:, cols], TN)
        state[1, 2 * hd] = st[:PROWS]
        state[1, 2 * hd + 1] = st[PROWS:]
    near_send(1)

    def local_work(hd):
        cols = slice(hd * HD, (hd + 1) * HD)
        half = ROWS // 2
        for tb in range(2):
            rows = slice(tb * half, (tb + 1) * half)
            width = (tb + 1) * half
            sc, gr = scaled_s[rows, cols], g_ref[rows, cols]
            ke, va = k_ref[:width, cols], v_ref[:width, cols]
            col = base + lax.broadcasted_iota(jnp.int32, (half, width), 1)
            row = base + tb * half + lax.broadcasted_iota(jnp.int32, (half, width), 0)
            first = jnp.tile(doc_start[rows], (1, width // HD))
            allowed = (col <= row) & (col >= first)
            w = jnp.where(allowed, dot(sc, ke, NT), 0.0).astype(BF16)
            dw = jnp.where(allowed, dot(gr, va, NT), 0.0).astype(BF16)
            acc[0, rows, cols] = dot(w, va, NN)
            acc[1, rows, cols] = dot(dw, ke, NN)
            gk, gv = dot(dw, sc, TN), dot(w, gr, TN)
            if tb == 0:
                acc[2, rows, cols] = gk
                acc[3, rows, cols] = gv
            else:
                acc[2, :half, cols] += gk[:half]
                acc[3, :half, cols] += gv[:half]
                acc[2, half:, cols] = gk[half:]
                acc[3, half:, cols] = gv[half:]

    local_work(0)

    block0 = grp * GROUP
    gbase = block0 * ROWS
    gend = gbase + GROUP * ROWS
    glast_start = start_of(gend - 1)
    gfirst_end = end_of(gbase)

    def far_copy(scan, d):
        return pltpu.make_async_remote_copy(
            far_out.at[scan], far_in.at[scan, d - 1], ss2.at[scan, d - 1], rs2.at[scan, d - 1],
            device_id=far(d if scan == 0 else -d), device_id_type=MESH)

    def far_send(scan, is_later):
        for d in (2, 1, 3, 4):
            @pl.when(later[scan][d - 1] == is_later)
            def _():
                if is_later:
                    pl.semaphore_wait(ready.at[scan, d - 1], 1)
                far_copy(scan, d).start()

    near_wait(0)
    total = near_in[0, GROUP - 1]
    for i in range(GROUP - 1):
        total += flag(glast_start < gbase + (i + 1) * ROWS) * near_in[0, i]
    far_out[0] = total
    far_send(0, 0)

    near_wait(1)
    total = near_in[1, 0]
    for i in range(1, GROUP):
        total += flag(gfirst_end > gbase + i * ROWS) * near_in[1, i]
    far_out[1] = total
    far_send(1, 0)

    local_work(1)

    far_send(0, 1)
    far_send(1, 1)

    gfirst_start = start_of(gbase)
    glast_end = end_of(gend - 1)

    def back_copy(scan, i, slot):
        return pltpu.make_async_remote_copy(
            back_out.at[scan, i], back_in.at[scan, slot], ss3.at[scan, i], rs3.at[scan, slot],
            device_id=member(i), device_id_type=MESH)

    def back_send(scan):
        for d in (2, 3, 1):
            back_copy(scan, (me + d) % GROUP, piece).start()
        back_in[scan, piece] = back_out[scan, me]

    def back_wait(scan):
        for d in (1, 2, 3):
            i = (me + d) % GROUP
            back_copy(scan, i, owner(grp, i)).wait_recv()

    for d in range(1, REACH + 1):
        far_copy(0, d).wait_recv()
    outer = flag(gfirst_start < gbase) * far_in[0, 0]
    for d in range(2, REACH + 1):
        outer += flag(gfirst_start < gbase - (d - 1) * GROUP * ROWS) * far_in[0, d - 1]
    for i in range(GROUP):
        begin = start_of(gbase + i * ROWS)
        entering = flag(begin < gbase) * outer
        for r in range(i):
            entering += flag(begin < gbase + (r + 1) * ROWS) * near_in[0, r]
        back_out[0, i] = entering
    back_send(0)

    for d in range(1, REACH + 1):
        far_copy(1, d).wait_recv()
    outer = flag(glast_end > gend) * far_in[1, 0]
    for d in range(2, REACH + 1):
        outer += flag(glast_end > gbase + d * GROUP * ROWS) * far_in[1, d - 1]
    for i in range(GROUP):
        finish = end_of(gbase + (i + 1) * ROWS - 1)
        returning = flag(finish > gend) * outer
        for r in range(i + 1, GROUP):
            returning += flag(finish > gbase + r * ROWS) * near_in[1, r]
        back_out[1, i] = returning
    back_send(1)

    back_wait(0)
    for hd in range(HEADS):
        cols = slice(hd * HD, (hd + 1) * HD)
        e_hi, e_lo = split(jnp.concatenate([back_in[0, 2 * hd], back_in[0, 2 * hd + 1]], axis=0))
        sc, gr = scaled_s[:, cols], g_ref[:, cols]
        att = acc[0, :, cols] + dot(sc, e_hi, NN) + dot(sc, e_lo, NN)
        att_ref[:, cols] = att.astype(BF16)
        gq = acc[1, :, cols] + dot(gr, e_hi, NT) + dot(gr, e_lo, NT)
        gq_ref[:, cols] = (row_scale * gq).astype(BF16)
    back_wait(1)
    for hd in range(HEADS):
        cols = slice(hd * HD, (hd + 1) * HD)
        r_hi, r_lo = split(jnp.concatenate([back_in[1, 2 * hd], back_in[1, 2 * hd + 1]], axis=0))
        ke, va = k_ref[:, cols], v_ref[:, cols]
        gk = acc[2, :, cols] + dot(va, r_hi, NT) + dot(va, r_lo, NT)
        gk_ref[:, cols] = gk.astype(BF16)
        gv = acc[3, :, cols] + dot(ke, r_hi, NN) + dot(ke, r_lo, NN)
        gv_ref[:, cols] = gv.astype(BF16)

    for scan in range(2):
        for d in range(1, GROUP):
            i = (me + d) % GROUP
            near_copy(scan, i, i).wait_send()
            back_copy(scan, i, i).wait_send()
        for d in range(1, REACH + 1):
            far_copy(scan, d).wait_send()


def writer(*refs):
    srcs, dsts, sem = refs[:4], refs[4:8], refs[8]
    copies = [pltpu.make_async_copy(a, b, sem.at[i]) for i, (a, b) in enumerate(zip(srcs, dsts))]
    for copy in copies:
        copy.start()
    for copy in copies:
        copy.wait()


def body(query_rows, key_rows, value_rows, out_grad, doc_lengths):
    vmem = pl.BlockSpec(memory_space=pltpu.VMEM)
    out = jax.ShapeDtypeStruct((ROWS, HEADS * HD), BF16)
    dma = pltpu.SemaphoreType.DMA
    hbm = pl.BlockSpec(memory_space=pltpu.HBM)
    rows = pltpu.VMEM((ROWS, HEADS * HD), BF16)
    results = pl.pallas_call(
        kernel,
        out_shape=(pltpu.VMEM((ROWS, HEADS * HD), BF16),) * 4,
        in_specs=[hbm] * 5,
        out_specs=(vmem,) * 4,
        scratch_shapes=[
            pltpu.SMEM((DOCS,), jnp.int32), rows, rows, rows, rows,
            pltpu.VMEM((2, PIECES, PROWS, HD), F32),
            pltpu.VMEM((2, GROUP, PROWS, HD), F32),
            pltpu.VMEM((2, PROWS, HD), F32),
            pltpu.VMEM((2, REACH, PROWS, HD), F32),
            pltpu.VMEM((2, GROUP, PROWS, HD), F32),
            pltpu.VMEM((2, PIECES, PROWS, HD), F32),
            pltpu.VMEM((ROWS, HEADS * HD), BF16),
            pltpu.VMEM((4, ROWS, HEADS * HD), F32),
            dma((5,)), pltpu.SemaphoreType.REGULAR((2, REACH)), dma((2, GROUP)), dma((2, GROUP)), dma((2, REACH)), dma((2, REACH)),
            dma((2, GROUP)), dma((2, GROUP)),
        ],
        compiler_params=pltpu.CompilerParams(
            collective_id=0, has_side_effects=True),
        name="linear_attention",
    )(doc_lengths, query_rows, key_rows, value_rows, out_grad)
    return pl.pallas_call(
        writer,
        out_shape=(out,) * 4,
        in_specs=[vmem] * 4,
        out_specs=(hbm,) * 4,
        scratch_shapes=[dma((4,))],
        name="write_out",
    )(*[pltpu.with_memory_space_constraint(x, pltpu.VMEM) for x in results])


def solution(mesh):
    in_specs = (P("ctx", "head"), P("ctx", "head"), P("ctx", "head"), P("ctx", "head"), P("head"))
    out_specs = (P("ctx", "head"), P("ctx", "head"), P("ctx", "head"), P("ctx", "head"))
    return jax.shard_map(body, mesh=mesh, in_specs=in_specs, out_specs=out_specs, check_vma=False)
```

```python
import functools

import jax
import jax.numpy as jnp
from jax import lax
from jax.experimental import pallas as pl
from jax.experimental.pallas import tpu as pltpu
from jax.sharding import PartitionSpec as P

HD = 128
HEADS = 2
ROWS = 512
DOCS = 8
BLOCKS = 64
GROUP = 4
GROUPS = BLOCKS // GROUP
REACH = 4
GROUP_COLS = 4
FAR = [(scan, d) for d in range(1, REACH + 1) for scan in range(2)]
PIECES = 4
PROWS = HEADS * HD // PIECES
MESH = pl.DeviceIdType.MESH
F32 = jnp.float32
BF16 = jnp.bfloat16
TN = (((0,), (0,)), ((), ()))
NT = (((1,), (1,)), ((), ()))
NN = (((1,), (0,)), ((), ()))


def dot(a, b, dims):
    return lax.dot_general(a, b, dims, preferred_element_type=F32)


def flag(cond):
    return jnp.where(cond, jnp.float32(1.0), jnp.float32(0.0))


def owner(group, piece):
    turned = (group % 4) // 2
    return piece + turned * (3 - 2 * piece)


def entry_order(group):
    column = group % GROUP_COLS
    place = column + (column // 2) * (5 - 2 * column)
    return place * (GROUPS // GROUP_COLS) + group // GROUP_COLS


def split(x):
    hi = x.astype(BF16)
    return hi, (x - hi.astype(F32)).astype(BF16)


def kernel(
    dl_hbm, q_hbm, k_hbm, v_hbm, g_hbm,
    att_ref, gq_ref, gk_acc, gv_acc, ret_ref, k_ref, v_ref,
    dl_ref, q_ref, g_ref,
    state, near_in, far_out, far_in, back_out, back_in, scaled_s, acc,
    ld, ready, ss1, rs1, ss2, rs2, ss3, rs3,
):
    loads = [
        pltpu.make_async_copy(src, dst, ld.at[i])
        for i, (src, dst) in enumerate(
            [(dl_hbm, dl_ref), (k_hbm, k_ref), (v_hbm, v_ref), (q_hbm, q_ref), (g_hbm, g_ref)])
    ]
    for load in loads:
        load.start()

    c = lax.axis_index("ctx")
    h = lax.axis_index("head")
    grp = c // GROUP
    me = c % GROUP
    piece = owner(grp, me)

    def member(i):
        return (grp * GROUP + i, h)

    def far(step):
        other = (grp + step + GROUPS) % GROUPS
        return (other * GROUP + owner(other, piece), h)

    def after(step):
        other = grp + step
        turn = jnp.where(entry_order((other + GROUPS) % GROUPS) > entry_order(grp), 1, 0)
        return jnp.where((other >= 0) & (other < GROUPS), turn, 2)

    later = [[after(d if scan == 0 else -d) for d in range(1, REACH + 1)] for scan in range(2)]

    far_in[...] = jnp.zeros_like(far_in)
    barrier = pltpu.get_barrier_semaphore()
    awaited = jnp.int32(GROUP - 1)
    for d in range(1, GROUP):
        pl.semaphore_signal(barrier, inc=1, device_id=member((me + d) % GROUP), device_id_type=MESH)
    for scan, d in FAR:
        awaited = awaited + jnp.where(later[scan][d - 1] == 0, 1, 0)

        @pl.when(later[scan][d - 1] == 1)
        def _():
            pl.semaphore_signal(
                barrier, inc=1, device_id=far(d if scan == 0 else -d), device_id_type=MESH)

    loads[0].wait()
    starts, ends = [], []
    total = jnp.int32(0)
    for d in range(DOCS):
        starts.append(total)
        total = total + dl_ref[d]
        ends.append(total)

    def start_of(pos):
        best = jnp.int32(0)
        for d in range(1, DOCS):
            best = jnp.where(starts[d] <= pos, starts[d], best)
        return best

    def end_of(pos):
        best = ends[DOCS - 1]
        for d in range(DOCS - 2, -1, -1):
            best = jnp.where(ends[d] > pos, ends[d], best)
        return best

    base = c * ROWS
    last_start = start_of(base + ROWS - 1)
    first_end = end_of(base)
    pos = base + lax.broadcasted_iota(jnp.int32, (ROWS, HD), 0)
    doc_start = jnp.zeros((ROWS, HD), jnp.int32)
    for d in range(1, DOCS):
        doc_start = jnp.where(pos >= starts[d], starts[d], doc_start)
    row_scale = lax.rsqrt((pos - doc_start).astype(F32) + 1.0) * HD ** (-0.5)
    in_last = pos >= last_start
    in_first = pos < first_end

    def near_copy(scan, i, slot):
        return pltpu.make_async_remote_copy(
            state.at[scan, owner(grp, i)], near_in.at[scan, slot], ss1.at[scan, i], rs1.at[scan, slot],
            device_id=member(i), device_id_type=MESH)

    def near_send(scan):
        for d in (2, 3, 1):
            near_copy(scan, (me + d) % GROUP, me).start()
        near_in[scan, me] = state[scan, piece]

    def near_wait(scan):
        for d in (1, 2, 3):
            i = (me + d) % GROUP
            near_copy(scan, i, i).wait_recv()

    loads[1].wait()
    loads[2].wait()
    for hd in range(HEADS):
        cols = slice(hd * HD, (hd + 1) * HD)
        tail = jnp.where(in_last, k_ref[:, cols].astype(F32), 0.0).astype(BF16)
        st = dot(tail, v_ref[:, cols], TN)
        state[0, 2 * hd] = st[:PROWS]
        state[0, 2 * hd + 1] = st[PROWS:]
    pl.semaphore_wait(barrier, awaited)
    near_send(0)
    for scan, d in FAR:
        @pl.when(later[scan][d - 1] == 0)
        def _():
            pl.semaphore_signal(
                ready.at[1 - scan, d - 1], inc=1,
                device_id=far(d if scan == 0 else -d), device_id_type=MESH)

    loads[3].wait()
    loads[4].wait()
    for hd in range(HEADS):
        cols = slice(hd * HD, (hd + 1) * HD)
        sc = q_ref[:, cols].astype(F32) * row_scale
        scaled_s[:, cols] = sc.astype(BF16)
        head = jnp.where(in_first, sc, 0.0).astype(BF16)
        st = dot(head, g_ref[:, cols], TN)
        state[1, 2 * hd] = st[:PROWS]
        state[1, 2 * hd + 1] = st[PROWS:]
    near_send(1)

    def local_work(hd):
        cols = slice(hd * HD, (hd + 1) * HD)
        half = ROWS // 2
        for tb in range(2):
            rows = slice(tb * half, (tb + 1) * half)
            width = (tb + 1) * half
            sc, gr = scaled_s[rows, cols], g_ref[rows, cols]
            ke, va = k_ref[:width, cols], v_ref[:width, cols]
            col = base + lax.broadcasted_iota(jnp.int32, (half, width), 1)
            row = base + tb * half + lax.broadcasted_iota(jnp.int32, (half, width), 0)
            first = jnp.tile(doc_start[rows], (1, width // HD))
            allowed = (col <= row) & (col >= first)
            w = jnp.where(allowed, dot(sc, ke, NT), 0.0).astype(BF16)
            dw = jnp.where(allowed, dot(gr, va, NT), 0.0).astype(BF16)
            acc[0, rows, cols] = dot(w, va, NN)
            acc[1, rows, cols] = dot(dw, ke, NN)
            gk, gv = dot(dw, sc, TN), dot(w, gr, TN)
            if tb == 0:
                gk_acc[rows, cols] = gk
                gv_acc[rows, cols] = gv
            else:
                gk_acc[:half, cols] += gk[:half]
                gv_acc[:half, cols] += gv[:half]
                gk_acc[half:, cols] = gk[half:]
                gv_acc[half:, cols] = gv[half:]

    local_work(0)

    block0 = grp * GROUP
    gbase = block0 * ROWS
    gend = gbase + GROUP * ROWS
    glast_start = start_of(gend - 1)
    gfirst_end = end_of(gbase)

    def far_copy(scan, d):
        return pltpu.make_async_remote_copy(
            far_out.at[scan], far_in.at[scan, d - 1], ss2.at[scan, d - 1], rs2.at[scan, d - 1],
            device_id=far(d if scan == 0 else -d), device_id_type=MESH)

    def far_send(scan, is_later):
        for d in (2, 1, 3, 4):
            @pl.when(later[scan][d - 1] == is_later)
            def _():
                if is_later:
                    pl.semaphore_wait(ready.at[scan, d - 1], 1)
                far_copy(scan, d).start()

    def far_wait(scan):
        for d in (4, 1, 3, 2):
            @pl.when(later[1 - scan][d - 1] < 2)
            def _():
                far_copy(scan, d).wait_recv()

    tail_on = [flag(glast_start < gbase + (i + 1) * ROWS) for i in range(GROUP - 1)]
    head_on = [flag(gfirst_end > gbase + i * ROWS) for i in range(1, GROUP)]
    near_wait(0)
    total = near_in[0, GROUP - 1]
    for i in range(GROUP - 1):
        total += tail_on[i] * near_in[0, i]
    far_out[0] = total
    far_send(0, 0)

    near_wait(1)
    total = near_in[1, 0]
    for i in range(1, GROUP):
        total += head_on[i - 1] * near_in[1, i]
    far_out[1] = total
    far_send(1, 0)

    local_work(1)

    gfirst_start = start_of(gbase)
    glast_end = end_of(gend - 1)
    left_on = [flag(gfirst_start < gbase - (d - 1) * GROUP * ROWS) for d in range(1, REACH + 1)]
    right_on = [flag(glast_end > gbase + d * GROUP * ROWS) for d in range(1, REACH + 1)]
    open_left, open_right = [], []
    for i in range(GROUP):
        begin = start_of(gbase + i * ROWS)
        finish = end_of(gbase + (i + 1) * ROWS - 1)
        open_left.append(flag(begin < gbase))
        open_right.append(flag(finish > gend))
        inside = jnp.zeros((PROWS, HD), F32)
        for r in range(i):
            inside += flag(begin < gbase + (r + 1) * ROWS) * near_in[0, r]
        back_out[0, i] = inside
        inside = jnp.zeros((PROWS, HD), F32)
        for r in range(i + 1, GROUP):
            inside += flag(finish > gbase + r * ROWS) * near_in[1, r]
        back_out[1, i] = inside

    far_send(0, 1)
    far_send(1, 1)

    def back_copy(scan, i, slot):
        return pltpu.make_async_remote_copy(
            back_out.at[scan, i], back_in.at[scan, slot], ss3.at[scan, i], rs3.at[scan, slot],
            device_id=member(i), device_id_type=MESH)

    def back_send(scan):
        for d in (2, 3, 1):
            back_copy(scan, (me + d) % GROUP, piece).start()
        back_in[scan, piece] = back_out[scan, me]

    def back_wait(scan):
        for d in (1, 2, 3):
            i = (me + d) % GROUP
            back_copy(scan, i, owner(grp, i)).wait_recv()

    far_wait(0)
    outer = left_on[0] * far_in[0, 0]
    for d in range(1, REACH):
        outer += left_on[d] * far_in[0, d]
    for i in range(GROUP):
        back_out[0, i] += open_left[i] * outer
    back_send(0)

    far_wait(1)
    outer = right_on[0] * far_in[1, 0]
    for d in range(1, REACH):
        outer += right_on[d] * far_in[1, d]
    for i in range(GROUP):
        back_out[1, i] += open_right[i] * outer
    back_send(1)

    back_wait(0)
    for hd in range(HEADS):
        cols = slice(hd * HD, (hd + 1) * HD)
        e_hi, e_lo = split(jnp.concatenate([back_in[0, 2 * hd], back_in[0, 2 * hd + 1]], axis=0))
        sc, gr = scaled_s[:, cols], g_ref[:, cols]
        att = acc[0, :, cols] + dot(sc, e_hi, NN) + dot(sc, e_lo, NN)
        att_ref[:, cols] = att.astype(BF16)
        gq = acc[1, :, cols] + dot(gr, e_hi, NT) + dot(gr, e_lo, NT)
        gq_ref[:, cols] = (row_scale * gq).astype(BF16)
    back_wait(1)
    ret_ref[...] = back_in[1]

    for scan in range(2):
        for d in range(1, GROUP):
            i = (me + d) % GROUP
            near_copy(scan, i, i).wait_send()
            back_copy(scan, i, i).wait_send()
        for d in range(1, REACH + 1):
            @pl.when(later[scan][d - 1] < 2)
            def _():
                far_copy(scan, d).wait_send()


def writer(att_ref, gq_ref, gk_acc, gv_acc, ret_ref, k_ref, v_ref, *rest):
    outs, gk_ref, gv_ref, sem = rest[:4], rest[4], rest[5], rest[6]
    copies = [pltpu.make_async_copy(src, dst, sem.at[i]) for i, (src, dst) in enumerate(zip((att_ref, gq_ref, gk_ref, gv_ref), outs))]
    copies[0].start()
    copies[1].start()
    r_all = [split(jnp.concatenate([ret_ref[2 * hd], ret_ref[2 * hd + 1]], axis=0)) for hd in range(HEADS)]
    for hd in range(HEADS):
        cols = slice(hd * HD, (hd + 1) * HD)
        gk = gk_acc[:, cols] + dot(v_ref[:, cols], r_all[hd][0], NT) + dot(v_ref[:, cols], r_all[hd][1], NT)
        gk_ref[:, cols] = gk.astype(BF16)
    copies[2].start()
    for hd in range(HEADS):
        cols = slice(hd * HD, (hd + 1) * HD)
        gv = gv_acc[:, cols] + dot(k_ref[:, cols], r_all[hd][0], NN) + dot(k_ref[:, cols], r_all[hd][1], NN)
        gv_ref[:, cols] = gv.astype(BF16)
    copies[3].start()
    for copy in copies:
        copy.wait()


def body(query_rows, key_rows, value_rows, out_grad, doc_lengths):
    vmem = pl.BlockSpec(memory_space=pltpu.VMEM)
    out = jax.ShapeDtypeStruct((ROWS, HEADS * HD), BF16)
    dma = pltpu.SemaphoreType.DMA
    hbm = pl.BlockSpec(memory_space=pltpu.HBM)
    rows = pltpu.VMEM((ROWS, HEADS * HD), BF16)
    wide = pltpu.VMEM((ROWS, HEADS * HD), F32)
    results = pl.pallas_call(
        kernel,
        out_shape=(rows, rows, wide, wide, pltpu.VMEM((PIECES, PROWS, HD), F32), rows, rows),
        in_specs=[hbm] * 5,
        out_specs=(vmem,) * 7,
        scratch_shapes=[
            pltpu.SMEM((DOCS,), jnp.int32), rows, rows,
            pltpu.VMEM((2, PIECES, PROWS, HD), F32),
            pltpu.VMEM((2, GROUP, PROWS, HD), F32),
            pltpu.VMEM((2, PROWS, HD), F32),
            pltpu.VMEM((2, REACH, PROWS, HD), F32),
            pltpu.VMEM((2, GROUP, PROWS, HD), F32),
            pltpu.VMEM((2, PIECES, PROWS, HD), F32),
            pltpu.VMEM((ROWS, HEADS * HD), BF16),
            pltpu.VMEM((2, ROWS, HEADS * HD), F32),
            dma((5,)), pltpu.SemaphoreType.REGULAR((2, REACH)), dma((2, GROUP)), dma((2, GROUP)), dma((2, REACH)), dma((2, REACH)),
            dma((2, GROUP)), dma((2, GROUP)),
        ],
        compiler_params=pltpu.CompilerParams(
            collective_id=0, has_side_effects=True),
        name="linear_attention",
    )(doc_lengths, query_rows, key_rows, value_rows, out_grad)
    return pl.pallas_call(
        writer,
        out_shape=(out,) * 4,
        in_specs=[vmem] * 7,
        out_specs=(hbm,) * 4,
        scratch_shapes=[rows, rows, dma((4,))],
        name="write_out",
    )(*[pltpu.with_memory_space_constraint(x, pltpu.VMEM) for x in results])


def solution(mesh):
    in_specs = (P("ctx", "head"), P("ctx", "head"), P("ctx", "head"), P("ctx", "head"), P("head"))
    out_specs = (P("ctx", "head"), P("ctx", "head"), P("ctx", "head"), P("ctx", "head"))
    return jax.shard_map(body, mesh=mesh, in_specs=in_specs, out_specs=out_specs, check_vma=False)
```

```python
import functools

import jax
import jax.numpy as jnp
from jax import lax
from jax.experimental import pallas as pl
from jax.experimental.pallas import tpu as pltpu
from jax.sharding import PartitionSpec as P

HD = 128
HEADS = 2
ROWS = 512
DOCS = 8
BLOCKS = 64
GROUP = 4
GROUPS = BLOCKS // GROUP
REACH = 4
GROUP_COLS = 4
FAR = [(scan, d) for d in range(1, REACH + 1) for scan in range(2)]
PIECES = 4
PROWS = HEADS * HD // PIECES
MESH = pl.DeviceIdType.MESH
F32 = jnp.float32
BF16 = jnp.bfloat16
TN = (((0,), (0,)), ((), ()))
NT = (((1,), (1,)), ((), ()))
NN = (((1,), (0,)), ((), ()))


def dot(a, b, dims):
    return lax.dot_general(a, b, dims, preferred_element_type=F32)


def flag(cond):
    return jnp.where(cond, jnp.float32(1.0), jnp.float32(0.0))


def owner(group, piece):
    turned = (group % 4) // 2
    return piece + turned * (3 - 2 * piece)


def entry_order(group):
    column = group % GROUP_COLS
    place = column + (column // 2) * (5 - 2 * column)
    return place * (GROUPS // GROUP_COLS) + group // GROUP_COLS


def split(x):
    hi = x.astype(BF16)
    return hi, (x - hi.astype(F32)).astype(BF16)


def kernel(
    dl_hbm, q_hbm, k_hbm, v_hbm, g_hbm,
    att_ref, gq_ref, gk_acc, gv_acc, ret_ref, k_ref, v_ref,
    dl_ref, q_ref, g_ref,
    state, near_in, far_out, far_in, back_out, back_in, scaled_s, acc,
    ld, ready, ss1, rs1, ss2, rs2, ss3, rs3,
):
    loads = [
        pltpu.make_async_copy(src, dst, ld.at[i])
        for i, (src, dst) in enumerate(
            [(dl_hbm, dl_ref), (k_hbm, k_ref), (v_hbm, v_ref), (q_hbm, q_ref), (g_hbm, g_ref)])
    ]
    for load in loads:
        load.start()

    c = lax.axis_index("ctx")
    h = lax.axis_index("head")
    grp = c // GROUP
    me = c % GROUP
    piece = owner(grp, me)

    def member(i):
        return (grp * GROUP + i, h)

    def far(step):
        other = (grp + step + GROUPS) % GROUPS
        return (other * GROUP + owner(other, piece), h)

    def after(step):
        other = grp + step
        turn = jnp.where(entry_order((other + GROUPS) % GROUPS) > entry_order(grp), 1, 0)
        return jnp.where((other >= 0) & (other < GROUPS), turn, 2)

    later = [[after(d if scan == 0 else -d) for d in range(1, REACH + 1)] for scan in range(2)]

    far_in[...] = jnp.zeros_like(far_in)
    barrier = pltpu.get_barrier_semaphore()
    awaited = jnp.int32(GROUP - 1)
    for d in range(1, GROUP):
        pl.semaphore_signal(barrier, inc=1, device_id=member((me + d) % GROUP), device_id_type=MESH)
    for scan, d in FAR:
        awaited = awaited + jnp.where(later[scan][d - 1] == 0, 1, 0)

        @pl.when(later[scan][d - 1] == 1)
        def _():
            pl.semaphore_signal(
                barrier, inc=1, device_id=far(d if scan == 0 else -d), device_id_type=MESH)

    loads[0].wait()
    starts, ends = [], []
    total = jnp.int32(0)
    for d in range(DOCS):
        starts.append(total)
        total = total + dl_ref[d]
        ends.append(total)

    def start_of(pos):
        best = jnp.int32(0)
        for d in range(1, DOCS):
            best = jnp.where(starts[d] <= pos, starts[d], best)
        return best

    def end_of(pos):
        best = ends[DOCS - 1]
        for d in range(DOCS - 2, -1, -1):
            best = jnp.where(ends[d] > pos, ends[d], best)
        return best

    base = c * ROWS
    last_start = start_of(base + ROWS - 1)
    first_end = end_of(base)
    pos = base + lax.broadcasted_iota(jnp.int32, (ROWS, HD), 0)
    doc_start = jnp.zeros((ROWS, HD), jnp.int32)
    for d in range(1, DOCS):
        doc_start = jnp.where(pos >= starts[d], starts[d], doc_start)
    row_scale = lax.rsqrt((pos - doc_start).astype(F32) + 1.0) * HD ** (-0.5)
    in_last = pos >= last_start
    in_first = pos < first_end

    def near_copy(scan, i, slot):
        return pltpu.make_async_remote_copy(
            state.at[scan, owner(grp, i)], near_in.at[scan, slot], ss1.at[scan, i], rs1.at[scan, slot],
            device_id=member(i), device_id_type=MESH)

    def near_send(scan):
        for i in (1, 2, 0, 3):
            @pl.when(me != i)
            def _():
                near_copy(scan, i, me).start()
        near_in[scan, me] = state[scan, piece]

    def near_wait(scan):
        for d in (1, 2, 3):
            i = (me + d) % GROUP
            near_copy(scan, i, i).wait_recv()

    loads[1].wait()
    loads[2].wait()
    for hd in range(HEADS):
        cols = slice(hd * HD, (hd + 1) * HD)
        tail = jnp.where(in_last, k_ref[:, cols].astype(F32), 0.0).astype(BF16)
        st = dot(tail, v_ref[:, cols], TN)
        state[0, 2 * hd] = st[:PROWS]
        state[0, 2 * hd + 1] = st[PROWS:]
    pl.semaphore_wait(barrier, awaited)
    near_send(0)
    for scan, d in FAR:
        @pl.when(later[scan][d - 1] == 0)
        def _():
            pl.semaphore_signal(
                ready.at[1 - scan, d - 1], inc=1,
                device_id=far(d if scan == 0 else -d), device_id_type=MESH)

    loads[3].wait()
    loads[4].wait()
    for hd in range(HEADS):
        cols = slice(hd * HD, (hd + 1) * HD)
        sc = q_ref[:, cols].astype(F32) * row_scale
        scaled_s[:, cols] = sc.astype(BF16)
        head = jnp.where(in_first, sc, 0.0).astype(BF16)
        st = dot(head, g_ref[:, cols], TN)
        state[1, 2 * hd] = st[:PROWS]
        state[1, 2 * hd + 1] = st[PROWS:]
    near_send(1)

    def local_work(hd):
        cols = slice(hd * HD, (hd + 1) * HD)
        half = ROWS // 2
        for tb in range(2):
            rows = slice(tb * half, (tb + 1) * half)
            width = (tb + 1) * half
            sc, gr = scaled_s[rows, cols], g_ref[rows, cols]
            ke, va = k_ref[:width, cols], v_ref[:width, cols]
            col = base + lax.broadcasted_iota(jnp.int32, (half, width), 1)
            row = base + tb * half + lax.broadcasted_iota(jnp.int32, (half, width), 0)
            first = jnp.tile(doc_start[rows], (1, width // HD))
            allowed = (col <= row) & (col >= first)
            w = jnp.where(allowed, dot(sc, ke, NT), 0.0).astype(BF16)
            dw = jnp.where(allowed, dot(gr, va, NT), 0.0).astype(BF16)
            acc[0, rows, cols] = dot(w, va, NN)
            acc[1, rows, cols] = dot(dw, ke, NN)
            gk, gv = dot(dw, sc, TN), dot(w, gr, TN)
            if tb == 0:
                gk_acc[rows, cols] = gk
                gv_acc[rows, cols] = gv
            else:
                gk_acc[:half, cols] += gk[:half]
                gv_acc[:half, cols] += gv[:half]
                gk_acc[half:, cols] = gk[half:]
                gv_acc[half:, cols] = gv[half:]

    local_work(0)

    block0 = grp * GROUP
    gbase = block0 * ROWS
    gend = gbase + GROUP * ROWS
    col = grp % GROUP_COLS
    glast_start = start_of(gend - 1)
    gfirst_end = end_of(gbase)

    def far_copy(scan, d):
        return pltpu.make_async_remote_copy(
            far_out.at[scan], far_in.at[scan, d - 1], ss2.at[scan, d - 1], rs2.at[scan, d - 1],
            device_id=far(d if scan == 0 else -d), device_id_type=MESH)

    def far_send(scan, column):
        step = column - col if scan == 0 else col - column
        d = (step + 2 * GROUP_COLS - 1) % GROUP_COLS + 1
        turn = after(d if scan == 0 else -d)

        @pl.when(turn == 1)
        def _():
            pl.semaphore_wait(ready.at[scan, d - 1], 1)

        @pl.when(turn < 2)
        def _():
            far_copy(scan, d).start()

    def far_sent(scan, column):
        step = column - col if scan == 0 else col - column
        d = (step + 2 * GROUP_COLS - 1) % GROUP_COLS + 1

        @pl.when(after(d if scan == 0 else -d) < 2)
        def _():
            far_copy(scan, d).wait_send()

    def far_wait(scan):
        for d in (4, 1, 3, 2):
            @pl.when(later[1 - scan][d - 1] < 2)
            def _():
                far_copy(scan, d).wait_recv()

    tail_on = [flag(glast_start < gbase + (i + 1) * ROWS) for i in range(GROUP - 1)]
    head_on = [flag(gfirst_end > gbase + i * ROWS) for i in range(1, GROUP)]
    near_wait(0)
    total = near_in[0, GROUP - 1]
    for i in range(GROUP - 1):
        total += tail_on[i] * near_in[0, i]
    far_out[0] = total
    far_send(0, 0)

    near_wait(1)
    total = near_in[1, 0]
    for i in range(1, GROUP):
        total += head_on[i - 1] * near_in[1, i]
    far_out[1] = total
    far_send(1, 0)

    local_work(1)
    far_sent(0, 0)
    far_sent(1, 0)
    far_send(0, 1)
    far_send(1, 1)

    gfirst_start = start_of(gbase)
    glast_end = end_of(gend - 1)
    left_on = [flag(gfirst_start < gbase - (d - 1) * GROUP * ROWS) for d in range(1, REACH + 1)]
    right_on = [flag(glast_end > gbase + d * GROUP * ROWS) for d in range(1, REACH + 1)]
    open_left, open_right = [], []
    for i in range(GROUP):
        begin = start_of(gbase + i * ROWS)
        finish = end_of(gbase + (i + 1) * ROWS - 1)
        open_left.append(flag(begin < gbase))
        open_right.append(flag(finish > gend))
        inside = jnp.zeros((PROWS, HD), F32)
        for r in range(i):
            inside += flag(begin < gbase + (r + 1) * ROWS) * near_in[0, r]
        back_out[0, i] = inside
        inside = jnp.zeros((PROWS, HD), F32)
        for r in range(i + 1, GROUP):
            inside += flag(finish > gbase + r * ROWS) * near_in[1, r]
        back_out[1, i] = inside

    far_sent(0, 1)
    far_sent(1, 1)
    for column in (2, 3):
        far_send(0, column)
        far_send(1, column)

    def back_copy(scan, i, slot):
        return pltpu.make_async_remote_copy(
            back_out.at[scan, i], back_in.at[scan, slot], ss3.at[scan, i], rs3.at[scan, slot],
            device_id=member(i), device_id_type=MESH)

    def back_send(scan):
        for i in range(GROUP):
            @pl.when(me != i)
            def _():
                back_copy(scan, i, piece).start()
        back_in[scan, piece] = back_out[scan, me]

    def back_wait(scan):
        for d in (1, 2, 3):
            i = (me + d) % GROUP
            back_copy(scan, i, owner(grp, i)).wait_recv()

    far_wait(0)
    outer = left_on[0] * far_in[0, 0]
    for d in range(1, REACH):
        outer += left_on[d] * far_in[0, d]
    for i in range(GROUP):
        back_out[0, i] += open_left[i] * outer
    back_send(0)

    far_wait(1)
    outer = right_on[0] * far_in[1, 0]
    for d in range(1, REACH):
        outer += right_on[d] * far_in[1, d]
    for i in range(GROUP):
        back_out[1, i] += open_right[i] * outer
    back_send(1)

    back_wait(0)
    for hd in range(HEADS):
        cols = slice(hd * HD, (hd + 1) * HD)
        e_hi, e_lo = split(jnp.concatenate([back_in[0, 2 * hd], back_in[0, 2 * hd + 1]], axis=0))
        sc, gr = scaled_s[:, cols], g_ref[:, cols]
        att = acc[0, :, cols] + dot(sc, e_hi, NN) + dot(sc, e_lo, NN)
        att_ref[:, cols] = att.astype(BF16)
        gq = acc[1, :, cols] + dot(gr, e_hi, NT) + dot(gr, e_lo, NT)
        gq_ref[:, cols] = (row_scale * gq).astype(BF16)
    back_wait(1)
    ret_ref[...] = back_in[1]

    for scan in range(2):
        for d in range(1, GROUP):
            i = (me + d) % GROUP
            near_copy(scan, i, i).wait_send()
            back_copy(scan, i, i).wait_send()
        for column in (2, 3):
            far_sent(scan, column)


def writer(att_ref, gq_ref, gk_acc, gv_acc, ret_ref, k_ref, v_ref, *rest):
    outs, gk_ref, gv_ref, sem = rest[:4], rest[4], rest[5], rest[6]
    copies = [pltpu.make_async_copy(src, dst, sem.at[i]) for i, (src, dst) in enumerate(zip((att_ref, gq_ref, gk_ref, gv_ref), outs))]
    copies[0].start()
    copies[1].start()
    r_all = [split(jnp.concatenate([ret_ref[2 * hd], ret_ref[2 * hd + 1]], axis=0)) for hd in range(HEADS)]
    for hd in range(HEADS):
        cols = slice(hd * HD, (hd + 1) * HD)
        gk = gk_acc[:, cols] + dot(v_ref[:, cols], r_all[hd][0], NT) + dot(v_ref[:, cols], r_all[hd][1], NT)
        gk_ref[:, cols] = gk.astype(BF16)
    copies[2].start()
    for hd in range(HEADS):
        cols = slice(hd * HD, (hd + 1) * HD)
        gv = gv_acc[:, cols] + dot(k_ref[:, cols], r_all[hd][0], NN) + dot(k_ref[:, cols], r_all[hd][1], NN)
        gv_ref[:, cols] = gv.astype(BF16)
    copies[3].start()
    for copy in copies:
        copy.wait()


def body(query_rows, key_rows, value_rows, out_grad, doc_lengths):
    vmem = pl.BlockSpec(memory_space=pltpu.VMEM)
    out = jax.ShapeDtypeStruct((ROWS, HEADS * HD), BF16)
    dma = pltpu.SemaphoreType.DMA
    hbm = pl.BlockSpec(memory_space=pltpu.HBM)
    rows = pltpu.VMEM((ROWS, HEADS * HD), BF16)
    wide = pltpu.VMEM((ROWS, HEADS * HD), F32)
    results = pl.pallas_call(
        kernel,
        out_shape=(rows, rows, wide, wide, pltpu.VMEM((PIECES, PROWS, HD), F32), rows, rows),
        in_specs=[hbm] * 5,
        out_specs=(vmem,) * 7,
        scratch_shapes=[
            pltpu.SMEM((DOCS,), jnp.int32), rows, rows,
            pltpu.VMEM((2, PIECES, PROWS, HD), F32),
            pltpu.VMEM((2, GROUP, PROWS, HD), F32),
            pltpu.VMEM((2, PROWS, HD), F32),
            pltpu.VMEM((2, REACH, PROWS, HD), F32),
            pltpu.VMEM((2, GROUP, PROWS, HD), F32),
            pltpu.VMEM((2, PIECES, PROWS, HD), F32),
            pltpu.VMEM((ROWS, HEADS * HD), BF16),
            pltpu.VMEM((2, ROWS, HEADS * HD), F32),
            dma((5,)), pltpu.SemaphoreType.REGULAR((2, REACH)), dma((2, GROUP)), dma((2, GROUP)), dma((2, REACH)), dma((2, REACH)),
            dma((2, GROUP)), dma((2, GROUP)),
        ],
        compiler_params=pltpu.CompilerParams(
            collective_id=0, has_side_effects=True),
        name="linear_attention",
    )(doc_lengths, query_rows, key_rows, value_rows, out_grad)
    return pl.pallas_call(
        writer,
        out_shape=(out,) * 4,
        in_specs=[vmem] * 7,
        out_specs=(hbm,) * 4,
        scratch_shapes=[rows, rows, dma((4,))],
        name="write_out",
    )(*[pltpu.with_memory_space_constraint(x, pltpu.VMEM) for x in results])


def solution(mesh):
    in_specs = (P("ctx", "head"), P("ctx", "head"), P("ctx", "head"), P("ctx", "head"), P("head"))
    out_specs = (P("ctx", "head"), P("ctx", "head"), P("ctx", "head"), P("ctx", "head"))
    return jax.shard_map(body, mesh=mesh, in_specs=in_specs, out_specs=out_specs, check_vma=False)
```

```python
import functools

import jax
import jax.numpy as jnp
from jax import lax
from jax.experimental import pallas as pl
from jax.experimental.pallas import tpu as pltpu
from jax.sharding import PartitionSpec as P

HD = 128
HEADS = 2
ROWS = 512
DOCS = 8
BLOCKS = 64
GROUP = 4
GROUPS = BLOCKS // GROUP
REACH = 4
GROUP_COLS = 4
FAR = [(scan, d) for d in range(1, REACH + 1) for scan in range(2)]
PIECES = 4
PROWS = HEADS * HD // PIECES
MESH = pl.DeviceIdType.MESH
F32 = jnp.float32
BF16 = jnp.bfloat16
TN = (((0,), (0,)), ((), ()))
NT = (((1,), (1,)), ((), ()))
NN = (((1,), (0,)), ((), ()))


def dot(a, b, dims):
    return lax.dot_general(a, b, dims, preferred_element_type=F32)


def flag(cond):
    return jnp.where(cond, jnp.float32(1.0), jnp.float32(0.0))


def owner(group, piece):
    turned = (group % 4) // 2
    return piece + turned * (3 - 2 * piece)


def entry_order(group):
    column = group % GROUP_COLS
    place = column + (column // 2) * (5 - 2 * column)
    return place * (GROUPS // GROUP_COLS) + group // GROUP_COLS


def split(x):
    hi = x.astype(BF16)
    return hi, (x - hi.astype(F32)).astype(BF16)


def kernel(
    dl_hbm, q_hbm, k_hbm, v_hbm, g_hbm,
    att_ref, gq_ref, gk_acc, gv_acc, ret_ref, k_ref, v_ref,
    dl_ref, q_ref, g_ref,
    state, near_in, far_out, far_in, back_out, back_in, scaled_s, acc,
    ld, ready, ss1, rs1, ss2, rs2, ss3, rs3,
):
    loads = [
        pltpu.make_async_copy(src, dst, ld.at[i])
        for i, (src, dst) in enumerate(
            [(dl_hbm, dl_ref), (k_hbm, k_ref), (v_hbm, v_ref), (q_hbm, q_ref), (g_hbm, g_ref)])
    ]
    for load in loads:
        load.start()

    c = lax.axis_index("ctx")
    h = lax.axis_index("head")
    grp = c // GROUP
    me = c % GROUP
    piece = owner(grp, me)

    def member(i):
        return (grp * GROUP + i, h)

    def far(step):
        other = (grp + step + GROUPS) % GROUPS
        return (other * GROUP + owner(other, piece), h)

    def after(step):
        other = grp + step
        turn = jnp.where(entry_order((other + GROUPS) % GROUPS) > entry_order(grp), 1, 0)
        return jnp.where((other >= 0) & (other < GROUPS), turn, 2)

    later = [[after(d if scan == 0 else -d) for d in range(1, REACH + 1)] for scan in range(2)]

    far_in[...] = jnp.zeros_like(far_in)
    barrier = pltpu.get_barrier_semaphore()
    awaited = jnp.int32(GROUP - 1)
    for d in range(1, GROUP):
        pl.semaphore_signal(barrier, inc=1, device_id=member((me + d) % GROUP), device_id_type=MESH)
    for scan, d in FAR:
        awaited = awaited + jnp.where(later[scan][d - 1] == 0, 1, 0)

        @pl.when(later[scan][d - 1] == 1)
        def _():
            pl.semaphore_signal(
                barrier, inc=1, device_id=far(d if scan == 0 else -d), device_id_type=MESH)

    loads[0].wait()
    starts, ends = [], []
    total = jnp.int32(0)
    for d in range(DOCS):
        starts.append(total)
        total = total + dl_ref[d]
        ends.append(total)

    def start_of(pos):
        best = jnp.int32(0)
        for d in range(1, DOCS):
            best = jnp.where(starts[d] <= pos, starts[d], best)
        return best

    def end_of(pos):
        best = ends[DOCS - 1]
        for d in range(DOCS - 2, -1, -1):
            best = jnp.where(ends[d] > pos, ends[d], best)
        return best

    base = c * ROWS
    last_start = start_of(base + ROWS - 1)
    first_end = end_of(base)
    pos = base + lax.broadcasted_iota(jnp.int32, (ROWS, HD), 0)
    doc_start = jnp.zeros((ROWS, HD), jnp.int32)
    for d in range(1, DOCS):
        doc_start = jnp.where(pos >= starts[d], starts[d], doc_start)
    row_scale = lax.rsqrt((pos - doc_start).astype(F32) + 1.0) * HD ** (-0.5)
    in_last = pos >= last_start
    in_first = pos < first_end

    def near_copy(scan, i, slot):
        return pltpu.make_async_remote_copy(
            state.at[scan, owner(grp, i)], near_in.at[scan, slot], ss1.at[scan, i], rs1.at[scan, slot],
            device_id=member(i), device_id_type=MESH)

    def near_send(scan):
        for i in (1, 2, 0, 3):
            @pl.when(me != i)
            def _():
                near_copy(scan, i, me).start()
        near_in[scan, me] = state[scan, piece]

    def near_wait(scan):
        for d in (1, 2, 3):
            i = (me + d) % GROUP
            near_copy(scan, i, i).wait_recv()

    loads[1].wait()
    loads[2].wait()
    for hd in range(HEADS):
        cols = slice(hd * HD, (hd + 1) * HD)
        tail = jnp.where(in_last, k_ref[:, cols].astype(F32), 0.0).astype(BF16)
        st = dot(tail, v_ref[:, cols], TN)
        state[0, 2 * hd] = st[:PROWS]
        state[0, 2 * hd + 1] = st[PROWS:]
    pl.semaphore_wait(barrier, awaited)
    near_send(0)
    for scan, d in FAR:
        @pl.when(later[scan][d - 1] == 0)
        def _():
            pl.semaphore_signal(
                ready.at[1 - scan, d - 1], inc=1,
                device_id=far(d if scan == 0 else -d), device_id_type=MESH)

    loads[3].wait()
    loads[4].wait()
    for hd in range(HEADS):
        cols = slice(hd * HD, (hd + 1) * HD)
        sc = q_ref[:, cols].astype(F32) * row_scale
        scaled_s[:, cols] = sc.astype(BF16)
        head = jnp.where(in_first, sc, 0.0).astype(BF16)
        st = dot(head, g_ref[:, cols], TN)
        state[1, 2 * hd] = st[:PROWS]
        state[1, 2 * hd + 1] = st[PROWS:]
    near_send(1)

    def local_work(hd):
        cols = slice(hd * HD, (hd + 1) * HD)
        half = ROWS // 2
        for tb in range(2):
            rows = slice(tb * half, (tb + 1) * half)
            width = (tb + 1) * half
            sc, gr = scaled_s[rows, cols], g_ref[rows, cols]
            ke, va = k_ref[:width, cols], v_ref[:width, cols]
            col = base + lax.broadcasted_iota(jnp.int32, (half, width), 1)
            row = base + tb * half + lax.broadcasted_iota(jnp.int32, (half, width), 0)
            first = jnp.tile(doc_start[rows], (1, width // HD))
            allowed = (col <= row) & (col >= first)
            w = jnp.where(allowed, dot(sc, ke, NT), 0.0).astype(BF16)
            dw = jnp.where(allowed, dot(gr, va, NT), 0.0).astype(BF16)
            acc[0, rows, cols] = dot(w, va, NN)
            acc[1, rows, cols] = dot(dw, ke, NN)
            gk, gv = dot(dw, sc, TN), dot(w, gr, TN)
            if tb == 0:
                gk_acc[rows, cols] = gk
                gv_acc[rows, cols] = gv
            else:
                gk_acc[:half, cols] += gk[:half]
                gv_acc[:half, cols] += gv[:half]
                gk_acc[half:, cols] = gk[half:]
                gv_acc[half:, cols] = gv[half:]

    local_work(0)

    block0 = grp * GROUP
    gbase = block0 * ROWS
    gend = gbase + GROUP * ROWS
    col = grp % GROUP_COLS
    glast_start = start_of(gend - 1)
    gfirst_end = end_of(gbase)

    def far_copy(scan, d):
        return pltpu.make_async_remote_copy(
            far_out.at[scan], far_in.at[scan, d - 1], ss2.at[scan, d - 1], rs2.at[scan, d - 1],
            device_id=far(d if scan == 0 else -d), device_id_type=MESH)

    def far_send(scan, column):
        step = column - col if scan == 0 else col - column
        d = (step + 2 * GROUP_COLS - 1) % GROUP_COLS + 1
        turn = after(d if scan == 0 else -d)

        @pl.when(turn == 1)
        def _():
            pl.semaphore_wait(ready.at[scan, d - 1], 1)

        @pl.when(turn < 2)
        def _():
            far_copy(scan, d).start()

    def far_sent(scan, column):
        step = column - col if scan == 0 else col - column
        d = (step + 2 * GROUP_COLS - 1) % GROUP_COLS + 1

        @pl.when(after(d if scan == 0 else -d) < 2)
        def _():
            far_copy(scan, d).wait_send()

    def far_wait(scan):
        for d in (4, 1, 3, 2):
            @pl.when(later[1 - scan][d - 1] < 2)
            def _():
                far_copy(scan, d).wait_recv()

    tail_on = [flag(glast_start < gbase + (i + 1) * ROWS) for i in range(GROUP - 1)]
    head_on = [flag(gfirst_end > gbase + i * ROWS) for i in range(1, GROUP)]
    near_wait(0)
    total = near_in[0, GROUP - 1]
    for i in range(GROUP - 1):
        total += tail_on[i] * near_in[0, i]
    far_out[0] = total
    far_send(0, 0)

    near_wait(1)
    total = near_in[1, 0]
    for i in range(1, GROUP):
        total += head_on[i - 1] * near_in[1, i]
    far_out[1] = total
    far_send(1, 0)

    local_work(1)
    far_sent(0, 0)
    far_sent(1, 0)
    far_send(0, 1)
    far_send(1, 1)

    gfirst_start = start_of(gbase)
    glast_end = end_of(gend - 1)
    left_on = [flag(gfirst_start < gbase - (d - 1) * GROUP * ROWS) for d in range(1, REACH + 1)]
    right_on = [flag(glast_end > gbase + d * GROUP * ROWS) for d in range(1, REACH + 1)]
    open_left, open_right = [], []
    for i in range(GROUP):
        begin = start_of(gbase + i * ROWS)
        finish = end_of(gbase + (i + 1) * ROWS - 1)
        open_left.append(flag(begin < gbase))
        open_right.append(flag(finish > gend))
        inside = jnp.zeros((PROWS, HD), F32)
        for r in range(i):
            inside += flag(begin < gbase + (r + 1) * ROWS) * near_in[0, r]
        back_out[0, i] = inside
        inside = jnp.zeros((PROWS, HD), F32)
        for r in range(i + 1, GROUP):
            inside += flag(finish > gbase + r * ROWS) * near_in[1, r]
        back_out[1, i] = inside

    far_sent(0, 1)
    far_sent(1, 1)
    for scan in range(2):
        for column in (2, 3):
            far_send(scan, column)

    def back_copy(scan, i, slot):
        return pltpu.make_async_remote_copy(
            back_out.at[scan, i], back_in.at[scan, slot], ss3.at[scan, i], rs3.at[scan, slot],
            device_id=member(i), device_id_type=MESH)

    def back_send(scan):
        for i in range(GROUP):
            @pl.when(me != i)
            def _():
                back_copy(scan, i, piece).start()
        back_in[scan, piece] = back_out[scan, me]

    def back_wait(scan):
        for d in (1, 2, 3):
            i = (me + d) % GROUP
            back_copy(scan, i, owner(grp, i)).wait_recv()

    far_wait(0)
    outer = left_on[0] * far_in[0, 0]
    for d in range(1, REACH):
        outer += left_on[d] * far_in[0, d]
    for i in range(GROUP):
        back_out[0, i] += open_left[i] * outer
    back_send(0)

    far_wait(1)
    outer = right_on[0] * far_in[1, 0]
    for d in range(1, REACH):
        outer += right_on[d] * far_in[1, d]
    for i in range(GROUP):
        back_out[1, i] += open_right[i] * outer
    back_send(1)

    back_wait(0)
    for hd in range(HEADS):
        cols = slice(hd * HD, (hd + 1) * HD)
        e_hi, e_lo = split(jnp.concatenate([back_in[0, 2 * hd], back_in[0, 2 * hd + 1]], axis=0))
        sc, gr = scaled_s[:, cols], g_ref[:, cols]
        att = acc[0, :, cols] + dot(sc, e_hi, NN) + dot(sc, e_lo, NN)
        att_ref[:, cols] = att.astype(BF16)
        gq = acc[1, :, cols] + dot(gr, e_hi, NT) + dot(gr, e_lo, NT)
        gq_ref[:, cols] = (row_scale * gq).astype(BF16)
    for scan in range(2):
        for d in range(1, GROUP):
            i = (me + d) % GROUP
            near_copy(scan, i, i).wait_send()
            back_copy(scan, i, i).wait_send()
        for column in (2, 3):
            far_sent(scan, column)

    back_wait(1)
    ret_ref[...] = back_in[1]


def writer(att_ref, gq_ref, gk_acc, gv_acc, ret_ref, k_ref, v_ref, *rest):
    outs, gk_ref, gv_ref, sem = rest[:4], rest[4], rest[5], rest[6]
    copies = [pltpu.make_async_copy(src, dst, sem.at[i]) for i, (src, dst) in enumerate(zip((att_ref, gq_ref, gk_ref, gv_ref), outs))]
    copies[0].start()
    copies[1].start()
    r_all = [split(jnp.concatenate([ret_ref[2 * hd], ret_ref[2 * hd + 1]], axis=0)) for hd in range(HEADS)]
    for hd in range(HEADS):
        cols = slice(hd * HD, (hd + 1) * HD)
        gk = gk_acc[:, cols] + dot(v_ref[:, cols], r_all[hd][0], NT) + dot(v_ref[:, cols], r_all[hd][1], NT)
        gk_ref[:, cols] = gk.astype(BF16)
    copies[2].start()
    for hd in range(HEADS):
        cols = slice(hd * HD, (hd + 1) * HD)
        gv = gv_acc[:, cols] + dot(k_ref[:, cols], r_all[hd][0], NN) + dot(k_ref[:, cols], r_all[hd][1], NN)
        gv_ref[:, cols] = gv.astype(BF16)
    copies[3].start()
    for copy in copies:
        copy.wait()


def body(query_rows, key_rows, value_rows, out_grad, doc_lengths):
    vmem = pl.BlockSpec(memory_space=pltpu.VMEM)
    out = jax.ShapeDtypeStruct((ROWS, HEADS * HD), BF16)
    dma = pltpu.SemaphoreType.DMA
    hbm = pl.BlockSpec(memory_space=pltpu.HBM)
    rows = pltpu.VMEM((ROWS, HEADS * HD), BF16)
    wide = pltpu.VMEM((ROWS, HEADS * HD), F32)
    results = pl.pallas_call(
        kernel,
        out_shape=(rows, rows, wide, wide, pltpu.VMEM((PIECES, PROWS, HD), F32), rows, rows),
        in_specs=[hbm] * 5,
        out_specs=(vmem,) * 7,
        scratch_shapes=[
            pltpu.SMEM((DOCS,), jnp.int32), rows, rows,
            pltpu.VMEM((2, PIECES, PROWS, HD), F32),
            pltpu.VMEM((2, GROUP, PROWS, HD), F32),
            pltpu.VMEM((2, PROWS, HD), F32),
            pltpu.VMEM((2, REACH, PROWS, HD), F32),
            pltpu.VMEM((2, GROUP, PROWS, HD), F32),
            pltpu.VMEM((2, PIECES, PROWS, HD), F32),
            pltpu.VMEM((ROWS, HEADS * HD), BF16),
            pltpu.VMEM((2, ROWS, HEADS * HD), F32),
            dma((5,)), pltpu.SemaphoreType.REGULAR((2, REACH)), dma((2, GROUP)), dma((2, GROUP)), dma((2, REACH)), dma((2, REACH)),
            dma((2, GROUP)), dma((2, GROUP)),
        ],
        compiler_params=pltpu.CompilerParams(
            collective_id=0, has_side_effects=True),
        name="linear_attention",
    )(doc_lengths, query_rows, key_rows, value_rows, out_grad)
    return pl.pallas_call(
        writer,
        out_shape=(out,) * 4,
        in_specs=[vmem] * 7,
        out_specs=(hbm,) * 4,
        scratch_shapes=[rows, rows, dma((4,))],
        name="write_out",
    )(*[pltpu.with_memory_space_constraint(x, pltpu.VMEM) for x in results])


def solution(mesh):
    in_specs = (P("ctx", "head"), P("ctx", "head"), P("ctx", "head"), P("ctx", "head"), P("head"))
    out_specs = (P("ctx", "head"), P("ctx", "head"), P("ctx", "head"), P("ctx", "head"))
    return jax.shard_map(body, mesh=mesh, in_specs=in_specs, out_specs=out_specs, check_vma=False)
```

```python
import functools

import jax
import jax.numpy as jnp
from jax import lax
from jax.experimental import pallas as pl
from jax.experimental.pallas import tpu as pltpu
from jax.sharding import PartitionSpec as P

HD = 128
HEADS = 2
ROWS = 512
DOCS = 8
BLOCKS = 64
GROUP = 4
GROUPS = BLOCKS // GROUP
REACH = 4
GROUP_COLS = 4
FAR = [(scan, d) for d in range(1, REACH + 1) for scan in range(2)]
PIECES = 4
PROWS = HEADS * HD // PIECES
MESH = pl.DeviceIdType.MESH
F32 = jnp.float32
BF16 = jnp.bfloat16
TN = (((0,), (0,)), ((), ()))
NT = (((1,), (1,)), ((), ()))
NN = (((1,), (0,)), ((), ()))


def dot(a, b, dims):
    return lax.dot_general(a, b, dims, preferred_element_type=F32)


def flag(cond):
    return jnp.where(cond, jnp.float32(1.0), jnp.float32(0.0))


def owner(group, piece):
    turned = (group % 4) // 2
    return piece + turned * (3 - 2 * piece)


def entry_order(group):
    column = group % GROUP_COLS
    place = column + (column // 2) * (5 - 2 * column)
    return place * (GROUPS // GROUP_COLS) + group // GROUP_COLS


def split(x):
    hi = x.astype(BF16)
    return hi, (x - hi.astype(F32)).astype(BF16)


def kernel(
    dl_hbm, q_hbm, k_hbm, v_hbm, g_hbm,
    att_ref, gq_ref, gk_acc, gv_acc, ret_ref, k_ref, v_ref,
    dl_ref, q_ref, g_ref,
    state, near_in, far_out, far_in, back_out, back_in, scaled_s, acc,
    ld, ready, ss1, rs1, ss2, rs2, ss3, rs3,
):
    loads = [
        pltpu.make_async_copy(src, dst, ld.at[i])
        for i, (src, dst) in enumerate(
            [(dl_hbm, dl_ref), (k_hbm, k_ref), (v_hbm, v_ref), (q_hbm, q_ref), (g_hbm, g_ref)])
    ]
    for load in loads:
        load.start()

    c = lax.axis_index("ctx")
    h = lax.axis_index("head")
    grp = c // GROUP
    me = c % GROUP
    piece = owner(grp, me)

    def member(i):
        return (grp * GROUP + i, h)

    def far(step):
        other = (grp + step + GROUPS) % GROUPS
        return (other * GROUP + owner(other, piece), h)

    def after(step):
        other = grp + step
        turn = jnp.where(entry_order((other + GROUPS) % GROUPS) > entry_order(grp), 1, 0)
        return jnp.where((other >= 0) & (other < GROUPS), turn, 2)

    later = [[after(d if scan == 0 else -d) for d in range(1, REACH + 1)] for scan in range(2)]

    far_in[...] = jnp.zeros_like(far_in)
    barrier = pltpu.get_barrier_semaphore()
    awaited = jnp.int32(GROUP - 1)
    for d in range(1, GROUP):
        pl.semaphore_signal(barrier, inc=1, device_id=member((me + d) % GROUP), device_id_type=MESH)
    for scan, d in FAR:
        awaited = awaited + jnp.where(later[scan][d - 1] == 0, 1, 0)

        @pl.when(later[scan][d - 1] == 1)
        def _():
            pl.semaphore_signal(
                barrier, inc=1, device_id=far(d if scan == 0 else -d), device_id_type=MESH)

    loads[0].wait()
    starts, ends = [], []
    total = jnp.int32(0)
    for d in range(DOCS):
        starts.append(total)
        total = total + dl_ref[d]
        ends.append(total)

    def start_of(pos):
        best = jnp.int32(0)
        for d in range(1, DOCS):
            best = jnp.where(starts[d] <= pos, starts[d], best)
        return best

    def end_of(pos):
        best = ends[DOCS - 1]
        for d in range(DOCS - 2, -1, -1):
            best = jnp.where(ends[d] > pos, ends[d], best)
        return best

    base = c * ROWS
    last_start = start_of(base + ROWS - 1)
    first_end = end_of(base)
    pos = base + lax.broadcasted_iota(jnp.int32, (ROWS, HD), 0)
    in_last = pos >= last_start

    def near_copy(scan, i, slot):
        return pltpu.make_async_remote_copy(
            state.at[scan, owner(grp, i)], near_in.at[scan, slot], ss1.at[scan, i], rs1.at[scan, slot],
            device_id=member(i), device_id_type=MESH)

    def near_send(scan):
        for i in (1, 2, 0, 3):
            @pl.when(me != i)
            def _():
                near_copy(scan, i, me).start()
        near_in[scan, me] = state[scan, piece]

    def near_wait(scan):
        for d in (1, 2, 3):
            i = (me + d) % GROUP
            near_copy(scan, i, i).wait_recv()

    loads[1].wait()
    loads[2].wait()
    for hd in range(HEADS):
        cols = slice(hd * HD, (hd + 1) * HD)
        tail = jnp.where(in_last, k_ref[:, cols].astype(F32), 0.0).astype(BF16)
        st = dot(tail, v_ref[:, cols], TN)
        state[0, 2 * hd] = st[:PROWS]
        state[0, 2 * hd + 1] = st[PROWS:]
    pl.semaphore_wait(barrier, awaited)
    near_send(0)
    doc_start = jnp.zeros((ROWS, HD), jnp.int32)
    for d in range(1, DOCS):
        doc_start = jnp.where(pos >= starts[d], starts[d], doc_start)
    row_scale = lax.rsqrt((pos - doc_start).astype(F32) + 1.0) * HD ** (-0.5)
    in_first = pos < first_end
    loads[3].wait()
    loads[4].wait()
    for hd in range(HEADS):
        cols = slice(hd * HD, (hd + 1) * HD)
        sc = q_ref[:, cols].astype(F32) * row_scale
        scaled_s[:, cols] = sc.astype(BF16)
        head = jnp.where(in_first, sc, 0.0).astype(BF16)
        st = dot(head, g_ref[:, cols], TN)
        state[1, 2 * hd] = st[:PROWS]
        state[1, 2 * hd + 1] = st[PROWS:]
    near_send(1)
    for scan, d in FAR:
        @pl.when(later[scan][d - 1] == 0)
        def _():
            pl.semaphore_signal(
                ready.at[1 - scan, d - 1], inc=1,
                device_id=far(d if scan == 0 else -d), device_id_type=MESH)

    def local_work(hd):
        cols = slice(hd * HD, (hd + 1) * HD)
        half = ROWS // 2
        for tb in range(2):
            rows = slice(tb * half, (tb + 1) * half)
            width = (tb + 1) * half
            sc, gr = scaled_s[rows, cols], g_ref[rows, cols]
            ke, va = k_ref[:width, cols], v_ref[:width, cols]
            col = base + lax.broadcasted_iota(jnp.int32, (half, width), 1)
            row = base + tb * half + lax.broadcasted_iota(jnp.int32, (half, width), 0)
            first = jnp.tile(doc_start[rows], (1, width // HD))
            allowed = (col <= row) & (col >= first)
            w = jnp.where(allowed, dot(sc, ke, NT), 0.0).astype(BF16)
            dw = jnp.where(allowed, dot(gr, va, NT), 0.0).astype(BF16)
            acc[0, rows, cols] = dot(w, va, NN)
            acc[1, rows, cols] = dot(dw, ke, NN)
            gk, gv = dot(dw, sc, TN), dot(w, gr, TN)
            if tb == 0:
                gk_acc[rows, cols] = gk
                gv_acc[rows, cols] = gv
            else:
                gk_acc[:half, cols] += gk[:half]
                gv_acc[:half, cols] += gv[:half]
                gk_acc[half:, cols] = gk[half:]
                gv_acc[half:, cols] = gv[half:]

    local_work(0)

    block0 = grp * GROUP
    gbase = block0 * ROWS
    gend = gbase + GROUP * ROWS
    col = grp % GROUP_COLS
    glast_start = start_of(gend - 1)
    gfirst_end = end_of(gbase)

    def far_copy(scan, d):
        return pltpu.make_async_remote_copy(
            far_out.at[scan], far_in.at[scan, d - 1], ss2.at[scan, d - 1], rs2.at[scan, d - 1],
            device_id=far(d if scan == 0 else -d), device_id_type=MESH)

    def far_send(scan, column):
        step = column - col if scan == 0 else col - column
        d = (step + 2 * GROUP_COLS - 1) % GROUP_COLS + 1
        turn = after(d if scan == 0 else -d)

        @pl.when(turn == 1)
        def _():
            pl.semaphore_wait(ready.at[scan, d - 1], 1)

        @pl.when(turn < 2)
        def _():
            far_copy(scan, d).start()

    def far_sent(scan, column):
        step = column - col if scan == 0 else col - column
        d = (step + 2 * GROUP_COLS - 1) % GROUP_COLS + 1

        @pl.when(after(d if scan == 0 else -d) < 2)
        def _():
            far_copy(scan, d).wait_send()

    def far_wait(scan):
        for d in (4, 1, 3, 2):
            @pl.when(later[1 - scan][d - 1] < 2)
            def _():
                far_copy(scan, d).wait_recv()

    tail_on = [flag(glast_start < gbase + (i + 1) * ROWS) for i in range(GROUP - 1)]
    head_on = [flag(gfirst_end > gbase + i * ROWS) for i in range(1, GROUP)]
    near_wait(0)
    total = near_in[0, GROUP - 1]
    for i in range(GROUP - 1):
        total += tail_on[i] * near_in[0, i]
    far_out[0] = total
    far_send(0, 0)

    near_wait(1)
    total = near_in[1, 0]
    for i in range(1, GROUP):
        total += head_on[i - 1] * near_in[1, i]
    far_out[1] = total
    far_send(1, 0)

    local_work(1)
    far_sent(0, 0)
    far_sent(1, 0)
    far_send(0, 1)
    far_send(1, 1)

    gfirst_start = start_of(gbase)
    glast_end = end_of(gend - 1)
    left_on = [flag(gfirst_start < gbase - (d - 1) * GROUP * ROWS) for d in range(1, REACH + 1)]
    right_on = [flag(glast_end > gbase + d * GROUP * ROWS) for d in range(1, REACH + 1)]
    open_left, open_right = [], []
    for i in range(GROUP):
        begin = start_of(gbase + i * ROWS)
        finish = end_of(gbase + (i + 1) * ROWS - 1)
        open_left.append(flag(begin < gbase))
        open_right.append(flag(finish > gend))
        inside = jnp.zeros((PROWS, HD), F32)
        for r in range(i):
            inside += flag(begin < gbase + (r + 1) * ROWS) * near_in[0, r]
        back_out[0, i] = inside
        inside = jnp.zeros((PROWS, HD), F32)
        for r in range(i + 1, GROUP):
            inside += flag(finish > gbase + r * ROWS) * near_in[1, r]
        back_out[1, i] = inside

    far_sent(0, 1)
    far_sent(1, 1)
    for scan in range(2):
        for column in (2, 3):
            far_send(scan, column)

    def back_copy(scan, i, slot):
        return pltpu.make_async_remote_copy(
            back_out.at[scan, i], back_in.at[scan, slot], ss3.at[scan, i], rs3.at[scan, slot],
            device_id=member(i), device_id_type=MESH)

    def back_send(scan):
        for i in range(GROUP):
            @pl.when(me != i)
            def _():
                back_copy(scan, i, piece).start()
        back_in[scan, piece] = back_out[scan, me]

    def back_wait(scan):
        for d in (1, 2, 3):
            i = (me + d) % GROUP
            back_copy(scan, i, owner(grp, i)).wait_recv()

    far_wait(0)
    outer = left_on[0] * far_in[0, 0]
    for d in range(1, REACH):
        outer += left_on[d] * far_in[0, d]
    for i in range(GROUP):
        back_out[0, i] += open_left[i] * outer
    back_send(0)

    far_wait(1)
    outer = right_on[0] * far_in[1, 0]
    for d in range(1, REACH):
        outer += right_on[d] * far_in[1, d]
    for i in range(GROUP):
        back_out[1, i] += open_right[i] * outer
    back_send(1)

    back_wait(0)
    for hd in range(HEADS):
        cols = slice(hd * HD, (hd + 1) * HD)
        e_hi, e_lo = split(jnp.concatenate([back_in[0, 2 * hd], back_in[0, 2 * hd + 1]], axis=0))
        sc, gr = scaled_s[:, cols], g_ref[:, cols]
        att = acc[0, :, cols] + dot(sc, e_hi, NN) + dot(sc, e_lo, NN)
        att_ref[:, cols] = att.astype(BF16)
        gq = acc[1, :, cols] + dot(gr, e_hi, NT) + dot(gr, e_lo, NT)
        gq_ref[:, cols] = (row_scale * gq).astype(BF16)
    for scan in range(2):
        for d in range(1, GROUP):
            i = (me + d) % GROUP
            near_copy(scan, i, i).wait_send()
            back_copy(scan, i, i).wait_send()
        for column in (2, 3):
            far_sent(scan, column)

    back_wait(1)
    ret_ref[...] = back_in[1]


def writer(att_ref, gq_ref, gk_acc, gv_acc, ret_ref, k_ref, v_ref, *rest):
    outs, gk_ref, gv_ref, sem = rest[:4], rest[4], rest[5], rest[6]
    copies = [pltpu.make_async_copy(src, dst, sem.at[i]) for i, (src, dst) in enumerate(zip((att_ref, gq_ref, gk_ref, gv_ref), outs))]
    copies[0].start()
    copies[1].start()
    r_all = [split(jnp.concatenate([ret_ref[2 * hd], ret_ref[2 * hd + 1]], axis=0)) for hd in range(HEADS)]
    for hd in range(HEADS):
        cols = slice(hd * HD, (hd + 1) * HD)
        gk = gk_acc[:, cols] + dot(v_ref[:, cols], r_all[hd][0], NT) + dot(v_ref[:, cols], r_all[hd][1], NT)
        gk_ref[:, cols] = gk.astype(BF16)
    copies[2].start()
    for hd in range(HEADS):
        cols = slice(hd * HD, (hd + 1) * HD)
        gv = gv_acc[:, cols] + dot(k_ref[:, cols], r_all[hd][0], NN) + dot(k_ref[:, cols], r_all[hd][1], NN)
        gv_ref[:, cols] = gv.astype(BF16)
    copies[3].start()
    for copy in copies:
        copy.wait()


def body(query_rows, key_rows, value_rows, out_grad, doc_lengths):
    vmem = pl.BlockSpec(memory_space=pltpu.VMEM)
    out = jax.ShapeDtypeStruct((ROWS, HEADS * HD), BF16)
    dma = pltpu.SemaphoreType.DMA
    hbm = pl.BlockSpec(memory_space=pltpu.HBM)
    rows = pltpu.VMEM((ROWS, HEADS * HD), BF16)
    wide = pltpu.VMEM((ROWS, HEADS * HD), F32)
    results = pl.pallas_call(
        kernel,
        out_shape=(rows, rows, wide, wide, pltpu.VMEM((PIECES, PROWS, HD), F32), rows, rows),
        in_specs=[hbm] * 5,
        out_specs=(vmem,) * 7,
        scratch_shapes=[
            pltpu.SMEM((DOCS,), jnp.int32), rows, rows,
            pltpu.VMEM((2, PIECES, PROWS, HD), F32),
            pltpu.VMEM((2, GROUP, PROWS, HD), F32),
            pltpu.VMEM((2, PROWS, HD), F32),
            pltpu.VMEM((2, REACH, PROWS, HD), F32),
            pltpu.VMEM((2, GROUP, PROWS, HD), F32),
            pltpu.VMEM((2, PIECES, PROWS, HD), F32),
            pltpu.VMEM((ROWS, HEADS * HD), BF16),
            pltpu.VMEM((2, ROWS, HEADS * HD), F32),
            dma((5,)), pltpu.SemaphoreType.REGULAR((2, REACH)), dma((2, GROUP)), dma((2, GROUP)), dma((2, REACH)), dma((2, REACH)),
            dma((2, GROUP)), dma((2, GROUP)),
        ],
        compiler_params=pltpu.CompilerParams(
            collective_id=0, has_side_effects=True),
        name="linear_attention",
    )(doc_lengths, query_rows, key_rows, value_rows, out_grad)
    return pl.pallas_call(
        writer,
        out_shape=(out,) * 4,
        in_specs=[vmem] * 7,
        out_specs=(hbm,) * 4,
        scratch_shapes=[rows, rows, dma((4,))],
        name="write_out",
    )(*[pltpu.with_memory_space_constraint(x, pltpu.VMEM) for x in results])


def solution(mesh):
    in_specs = (P("ctx", "head"), P("ctx", "head"), P("ctx", "head"), P("ctx", "head"), P("head"))
    out_specs = (P("ctx", "head"), P("ctx", "head"), P("ctx", "head"), P("ctx", "head"))
    return jax.shard_map(body, mesh=mesh, in_specs=in_specs, out_specs=out_specs, check_vma=False)
```

```python
import functools

import jax
import jax.numpy as jnp
from jax import lax
from jax.experimental import pallas as pl
from jax.experimental.pallas import tpu as pltpu
from jax.sharding import PartitionSpec as P

HD = 128
HEADS = 2
ROWS = 512
DOCS = 8
BLOCKS = 64
GROUP = 4
GROUPS = BLOCKS // GROUP
REACH = 4
GROUP_COLS = 4
FAR = [(scan, d) for d in range(1, REACH + 1) for scan in range(2)]
PIECES = 4
PROWS = HEADS * HD // PIECES
MESH = pl.DeviceIdType.MESH
F32 = jnp.float32
BF16 = jnp.bfloat16
TN = (((0,), (0,)), ((), ()))
NT = (((1,), (1,)), ((), ()))
NN = (((1,), (0,)), ((), ()))


def dot(a, b, dims):
    return lax.dot_general(a, b, dims, preferred_element_type=F32)


def flag(cond):
    return jnp.where(cond, jnp.float32(1.0), jnp.float32(0.0))


def owner(group, piece):
    turned = (group % 4) // 2
    return piece + turned * (3 - 2 * piece)


def entry_order(group):
    column = group % GROUP_COLS
    place = column + (column // 2) * (5 - 2 * column)
    return place * (GROUPS // GROUP_COLS) + group // GROUP_COLS


def split(x):
    hi = x.astype(BF16)
    return hi, (x - hi.astype(F32)).astype(BF16)


def kernel(
    dl_hbm, q_hbm, k_hbm, v_hbm, g_hbm,
    att_ref, gq_ref, gk_acc, gv_acc, ret_ref, k_ref, v_ref,
    dl_ref, q_ref, g_ref,
    state, near_in, far_out, far_in, back_out, back_in, scaled_s, acc,
    ld, ready, ss1, rs1, ss2, rs2, ss3, rs3,
):
    loads = [
        pltpu.make_async_copy(src, dst, ld.at[i])
        for i, (src, dst) in enumerate(
            [(dl_hbm, dl_ref), (k_hbm, k_ref), (v_hbm, v_ref), (q_hbm, q_ref), (g_hbm, g_ref)])
    ]
    for load in loads:
        load.start()

    c = lax.axis_index("ctx")
    h = lax.axis_index("head")
    grp = c // GROUP
    me = c % GROUP
    piece = owner(grp, me)

    def member(i):
        return (grp * GROUP + i, h)

    def far(step):
        other = (grp + step + GROUPS) % GROUPS
        return (other * GROUP + owner(other, piece), h)

    def after(step):
        other = grp + step
        turn = jnp.where(entry_order((other + GROUPS) % GROUPS) > entry_order(grp), 1, 0)
        return jnp.where((other >= 0) & (other < GROUPS), turn, 2)

    later = [[after(d if scan == 0 else -d) for d in range(1, REACH + 1)] for scan in range(2)]

    barrier = pltpu.get_barrier_semaphore()
    for d in range(1, GROUP):
        pl.semaphore_signal(barrier, inc=1, device_id=member((me + d) % GROUP), device_id_type=MESH)
    far_in[...] = jnp.zeros_like(far_in)
    awaited = jnp.int32(GROUP - 1)
    for scan, d in FAR:
        awaited = awaited + jnp.where(later[scan][d - 1] == 0, 1, 0)

        @pl.when(later[scan][d - 1] == 1)
        def _():
            pl.semaphore_signal(
                barrier, inc=1, device_id=far(d if scan == 0 else -d), device_id_type=MESH)

    loads[0].wait()
    starts, ends = [], []
    total = jnp.int32(0)
    for d in range(DOCS):
        starts.append(total)
        total = total + dl_ref[d]
        ends.append(total)

    def start_of(pos):
        best = jnp.int32(0)
        for d in range(1, DOCS):
            best = jnp.where(starts[d] <= pos, starts[d], best)
        return best

    def end_of(pos):
        best = ends[DOCS - 1]
        for d in range(DOCS - 2, -1, -1):
            best = jnp.where(ends[d] > pos, ends[d], best)
        return best

    base = c * ROWS
    last_start = start_of(base + ROWS - 1)
    first_end = end_of(base)
    pos = base + lax.broadcasted_iota(jnp.int32, (ROWS, HD), 0)
    in_last = pos >= last_start

    def near_copy(scan, i, slot):
        return pltpu.make_async_remote_copy(
            state.at[scan, owner(grp, i)], near_in.at[scan, slot], ss1.at[scan, i], rs1.at[scan, slot],
            device_id=member(i), device_id_type=MESH)

    def near_send(scan):
        for i in (1, 2, 0, 3):
            @pl.when(me != i)
            def _():
                near_copy(scan, i, me).start()
        near_in[scan, me] = state[scan, piece]

    def near_wait(scan):
        for d in (1, 2, 3):
            i = (me + d) % GROUP
            near_copy(scan, i, i).wait_recv()

    loads[1].wait()
    loads[2].wait()
    for hd in range(HEADS):
        cols = slice(hd * HD, (hd + 1) * HD)
        tail = jnp.where(in_last, k_ref[:, cols].astype(F32), 0.0).astype(BF16)
        st = dot(tail, v_ref[:, cols], TN)
        state[0, 2 * hd] = st[:PROWS]
        state[0, 2 * hd + 1] = st[PROWS:]
    pl.semaphore_wait(barrier, awaited)
    near_send(0)
    doc_start = jnp.zeros((ROWS, HD), jnp.int32)
    for d in range(1, DOCS):
        doc_start = jnp.where(pos >= starts[d], starts[d], doc_start)
    row_scale = lax.rsqrt((pos - doc_start).astype(F32) + 1.0) * HD ** (-0.5)
    in_first = pos < first_end
    loads[3].wait()
    loads[4].wait()
    for hd in range(HEADS):
        cols = slice(hd * HD, (hd + 1) * HD)
        sc = q_ref[:, cols].astype(F32) * row_scale
        scaled_s[:, cols] = sc.astype(BF16)
        head = jnp.where(in_first, sc, 0.0).astype(BF16)
        st = dot(head, g_ref[:, cols], TN)
        state[1, 2 * hd] = st[:PROWS]
        state[1, 2 * hd + 1] = st[PROWS:]
    near_send(1)
    for scan, d in FAR:
        @pl.when(later[scan][d - 1] == 0)
        def _():
            pl.semaphore_signal(
                ready.at[1 - scan, d - 1], inc=1,
                device_id=far(d if scan == 0 else -d), device_id_type=MESH)

    def local_work(hd):
        cols = slice(hd * HD, (hd + 1) * HD)
        half = ROWS // 2
        for tb in range(2):
            rows = slice(tb * half, (tb + 1) * half)
            width = (tb + 1) * half
            sc, gr = scaled_s[rows, cols], g_ref[rows, cols]
            ke, va = k_ref[:width, cols], v_ref[:width, cols]
            col = base + lax.broadcasted_iota(jnp.int32, (half, width), 1)
            row = base + tb * half + lax.broadcasted_iota(jnp.int32, (half, width), 0)
            first = jnp.tile(doc_start[rows], (1, width // HD))
            allowed = (col <= row) & (col >= first)
            w = jnp.where(allowed, dot(sc, ke, NT), 0.0).astype(BF16)
            dw = jnp.where(allowed, dot(gr, va, NT), 0.0).astype(BF16)
            acc[0, rows, cols] = dot(w, va, NN)
            acc[1, rows, cols] = dot(dw, ke, NN)
            gk, gv = dot(dw, sc, TN), dot(w, gr, TN)
            if tb == 0:
                gk_acc[rows, cols] = gk
                gv_acc[rows, cols] = gv
            else:
                gk_acc[:half, cols] += gk[:half]
                gv_acc[:half, cols] += gv[:half]
                gk_acc[half:, cols] = gk[half:]
                gv_acc[half:, cols] = gv[half:]

    local_work(0)

    block0 = grp * GROUP
    gbase = block0 * ROWS
    gend = gbase + GROUP * ROWS
    col = grp % GROUP_COLS
    glast_start = start_of(gend - 1)
    gfirst_end = end_of(gbase)

    def far_copy(scan, d):
        return pltpu.make_async_remote_copy(
            far_out.at[scan], far_in.at[scan, d - 1], ss2.at[scan, d - 1], rs2.at[scan, d - 1],
            device_id=far(d if scan == 0 else -d), device_id_type=MESH)

    def far_send(scan, column):
        step = column - col if scan == 0 else col - column
        d = (step + 2 * GROUP_COLS - 1) % GROUP_COLS + 1
        turn = after(d if scan == 0 else -d)

        @pl.when(turn == 1)
        def _():
            pl.semaphore_wait(ready.at[scan, d - 1], 1)

        @pl.when(turn < 2)
        def _():
            far_copy(scan, d).start()

    def far_sent(scan, column):
        step = column - col if scan == 0 else col - column
        d = (step + 2 * GROUP_COLS - 1) % GROUP_COLS + 1

        @pl.when(after(d if scan == 0 else -d) < 2)
        def _():
            far_copy(scan, d).wait_send()

    def far_wait(scan):
        for d in (4, 1, 3, 2):
            @pl.when(later[1 - scan][d - 1] < 2)
            def _():
                far_copy(scan, d).wait_recv()

    tail_on = [flag(glast_start < gbase + (i + 1) * ROWS) for i in range(GROUP - 1)]
    head_on = [flag(gfirst_end > gbase + i * ROWS) for i in range(1, GROUP)]
    near_wait(0)
    total = near_in[0, GROUP - 1]
    for i in range(GROUP - 1):
        total += tail_on[i] * near_in[0, i]
    far_out[0] = total
    far_send(0, 0)

    near_wait(1)
    total = near_in[1, 0]
    for i in range(1, GROUP):
        total += head_on[i - 1] * near_in[1, i]
    far_out[1] = total
    far_send(1, 0)

    local_work(1)
    far_sent(0, 0)
    far_sent(1, 0)
    far_send(0, 1)
    far_send(1, 1)

    gfirst_start = start_of(gbase)
    glast_end = end_of(gend - 1)
    left_on = [flag(gfirst_start < gbase - (d - 1) * GROUP * ROWS) for d in range(1, REACH + 1)]
    right_on = [flag(glast_end > gbase + d * GROUP * ROWS) for d in range(1, REACH + 1)]
    open_left, open_right = [], []
    for i in range(GROUP):
        begin = start_of(gbase + i * ROWS)
        finish = end_of(gbase + (i + 1) * ROWS - 1)
        open_left.append(flag(begin < gbase))
        open_right.append(flag(finish > gend))
        inside = jnp.zeros((PROWS, HD), F32)
        for r in range(i):
            inside += flag(begin < gbase + (r + 1) * ROWS) * near_in[0, r]
        back_out[0, i] = inside
        inside = jnp.zeros((PROWS, HD), F32)
        for r in range(i + 1, GROUP):
            inside += flag(finish > gbase + r * ROWS) * near_in[1, r]
        back_out[1, i] = inside

    far_sent(0, 1)
    far_sent(1, 1)
    for scan in range(2):
        for column in (2, 3):
            far_send(scan, column)

    def back_copy(scan, i, slot):
        return pltpu.make_async_remote_copy(
            back_out.at[scan, i], back_in.at[scan, slot], ss3.at[scan, i], rs3.at[scan, slot],
            device_id=member(i), device_id_type=MESH)

    def back_send(scan):
        for i in range(GROUP):
            @pl.when(me != i)
            def _():
                back_copy(scan, i, piece).start()
        back_in[scan, piece] = back_out[scan, me]

    def back_wait(scan):
        for d in (1, 2, 3):
            i = (me + d) % GROUP
            back_copy(scan, i, owner(grp, i)).wait_recv()

    far_wait(0)
    outer = left_on[0] * far_in[0, 0]
    for d in range(1, REACH):
        outer += left_on[d] * far_in[0, d]
    for i in range(GROUP):
        back_out[0, i] += open_left[i] * outer
    back_send(0)

    far_wait(1)
    outer = right_on[0] * far_in[1, 0]
    for d in range(1, REACH):
        outer += right_on[d] * far_in[1, d]
    for i in range(GROUP):
        back_out[1, i] += open_right[i] * outer
    back_send(1)

    back_wait(0)
    for hd in range(HEADS):
        cols = slice(hd * HD, (hd + 1) * HD)
        e_hi, e_lo = split(jnp.concatenate([back_in[0, 2 * hd], back_in[0, 2 * hd + 1]], axis=0))
        sc, gr = scaled_s[:, cols], g_ref[:, cols]
        att = acc[0, :, cols] + dot(sc, e_hi, NN) + dot(sc, e_lo, NN)
        att_ref[:, cols] = att.astype(BF16)
        gq = acc[1, :, cols] + dot(gr, e_hi, NT) + dot(gr, e_lo, NT)
        gq_ref[:, cols] = (row_scale * gq).astype(BF16)
    for scan in range(2):
        for d in range(1, GROUP):
            i = (me + d) % GROUP
            near_copy(scan, i, i).wait_send()
            back_copy(scan, i, i).wait_send()
        for column in (2, 3):
            far_sent(scan, column)

    back_wait(1)
    ret_ref[...] = back_in[1]


def writer(att_ref, gq_ref, gk_acc, gv_acc, ret_ref, k_ref, v_ref, *rest):
    outs, gk_ref, gv_ref, sem = rest[:4], rest[4], rest[5], rest[6]
    copies = [pltpu.make_async_copy(src, dst, sem.at[i]) for i, (src, dst) in enumerate(zip((att_ref, gq_ref, gk_ref, gv_ref), outs))]
    copies[0].start()
    copies[1].start()
    r_all = [split(jnp.concatenate([ret_ref[2 * hd], ret_ref[2 * hd + 1]], axis=0)) for hd in range(HEADS)]
    for hd in range(HEADS):
        cols = slice(hd * HD, (hd + 1) * HD)
        gk = gk_acc[:, cols] + dot(v_ref[:, cols], r_all[hd][0], NT) + dot(v_ref[:, cols], r_all[hd][1], NT)
        gk_ref[:, cols] = gk.astype(BF16)
    copies[2].start()
    for hd in range(HEADS):
        cols = slice(hd * HD, (hd + 1) * HD)
        gv = gv_acc[:, cols] + dot(k_ref[:, cols], r_all[hd][0], NN) + dot(k_ref[:, cols], r_all[hd][1], NN)
        gv_ref[:, cols] = gv.astype(BF16)
    copies[3].start()
    for copy in copies:
        copy.wait()


def body(query_rows, key_rows, value_rows, out_grad, doc_lengths):
    vmem = pl.BlockSpec(memory_space=pltpu.VMEM)
    out = jax.ShapeDtypeStruct((ROWS, HEADS * HD), BF16)
    dma = pltpu.SemaphoreType.DMA
    hbm = pl.BlockSpec(memory_space=pltpu.HBM)
    rows = pltpu.VMEM((ROWS, HEADS * HD), BF16)
    wide = pltpu.VMEM((ROWS, HEADS * HD), F32)
    results = pl.pallas_call(
        kernel,
        out_shape=(rows, rows, wide, wide, pltpu.VMEM((PIECES, PROWS, HD), F32), rows, rows),
        in_specs=[hbm] * 5,
        out_specs=(vmem,) * 7,
        scratch_shapes=[
            pltpu.SMEM((DOCS,), jnp.int32), rows, rows,
            pltpu.VMEM((2, PIECES, PROWS, HD), F32),
            pltpu.VMEM((2, GROUP, PROWS, HD), F32),
            pltpu.VMEM((2, PROWS, HD), F32),
            pltpu.VMEM((2, REACH, PROWS, HD), F32),
            pltpu.VMEM((2, GROUP, PROWS, HD), F32),
            pltpu.VMEM((2, PIECES, PROWS, HD), F32),
            pltpu.VMEM((ROWS, HEADS * HD), BF16),
            pltpu.VMEM((2, ROWS, HEADS * HD), F32),
            dma((5,)), pltpu.SemaphoreType.REGULAR((2, REACH)), dma((2, GROUP)), dma((2, GROUP)), dma((2, REACH)), dma((2, REACH)),
            dma((2, GROUP)), dma((2, GROUP)),
        ],
        compiler_params=pltpu.CompilerParams(
            collective_id=0, has_side_effects=True),
        name="linear_attention",
    )(doc_lengths, query_rows, key_rows, value_rows, out_grad)
    return pl.pallas_call(
        writer,
        out_shape=(out,) * 4,
        in_specs=[vmem] * 7,
        out_specs=(hbm,) * 4,
        scratch_shapes=[rows, rows, dma((4,))],
        name="write_out",
    )(*[pltpu.with_memory_space_constraint(x, pltpu.VMEM) for x in results])


def solution(mesh):
    in_specs = (P("ctx", "head"), P("ctx", "head"), P("ctx", "head"), P("ctx", "head"), P("head"))
    out_specs = (P("ctx", "head"), P("ctx", "head"), P("ctx", "head"), P("ctx", "head"))
    return jax.shard_map(body, mesh=mesh, in_specs=in_specs, out_specs=out_specs, check_vma=False)
```
